32 devices in a mesh: shot: 8 (over z, y), xline: 4 (over x, core).
Axes of the slice: x: 2, y: 2, z: 4, core: 2. Of those that a mesh axis runs over, the one named last changes fastest.
Arguments:
- records: bfloat16 [4, 16, 256, 2048], P('xline', 'shot'), may hold values from -1.796875 to 1.796875
- targets: bfloat16 [2048, 32, 256], P('xline', 'shot'), may hold values from -1.796875 to 1.796875
- aperture: int32 [32, 4, 16], P('shot', 'xline'), may hold values from 0 to 255
Outputs:
- multiples: bfloat16 [2048, 32, 256], P('xline', 'shot')
The draws below stay inside these ranges and needn't reach their ends.
Inputs may be any that keep to these rules, and one draw needn't show every extreme that they name: An aperture entry is the receiver of the output shot at which the contributing source lies.
All inputs are finite; a program needn't handle non-finite values.
Results may differ from the reference program's by a relative error of at most 0.0071.
Values may be sent and summed in bfloat16 or wider, within the bound.
A program may use at most 128 MiB of HBM per device.

```python
import math
import jax
import jax.numpy as jnp
from jax import lax

R = 256
NT = 2048
NF = 256
NS = 32
NC = 16
NL = 4


def with_ends(result, key, low, high):
    dims = result.shape
    index_at = [jax.random.randint(jax.random.fold_in(key, axis), (), 0, dims[axis]) for axis in range(len(dims))]
    result = result.at[tuple(index_at)].set(low)
    longest = dims.index(max(dims))
    index_at[longest] = (index_at[longest] + 1) % dims[longest]
    return result.at[tuple(index_at)].set(high)


def level_of(rng, extent, shards, least, high):
    level = 1.0
    for dim, parts in shards:
        steps = jax.random.uniform(jax.random.fold_in(jax.random.fold_in(rng, 6), dim), (parts,), jnp.float32, least / len(shards), high / len(shards))
        level = level * jnp.repeat(jnp.exp(steps), extent[dim] // parts).reshape((-1,) + (1,) * (len(extent) - 1 - dim))
    return level


def gaussian(own_key, dims, deviation, bound, cuts=(), held_as=jnp.bfloat16):
    result = deviation * jax.random.normal(own_key, dims, jnp.float32)
    if cuts:
        result = result * level_of(own_key, dims, cuts, -0.22, 0.18)
    return jnp.clip(result, -bound, bound).astype(held_as)


def setup_inputs(seed: int = 0) -> dict:
    splits = jax.random.split(jax.random.key(seed), 4)
    records = gaussian(splits[0], (NL, NC, R, NT), 0.3, 1.796875, ((0, 4), (1, 8)))
    targets = gaussian(splits[1], (NT, NS, R), 0.3, 1.796875, ((0, 4), (1, 8)))
    aperture = with_ends(jax.random.randint(splits[2], (NS, NL, NC), 0, R), jax.random.fold_in(splits[2], 1), 0, R - 1).astype(jnp.int32)
    return dict(records=records, targets=targets, aperture=aperture)


def forward_table():
    times_col = jnp.arange(NT, dtype=jnp.int32)[:, None]
    freq_row = jnp.arange(1, NF + 1, dtype=jnp.int32)[None, :]
    angles = (times_col * freq_row % NT).astype(jnp.float32) * (2.0 * math.pi / NT)
    normalizing_scale = 1.0 / math.sqrt(NT)
    return jnp.concatenate([jnp.cos(angles) * normalizing_scale, -jnp.sin(angles) * normalizing_scale], axis=1).astype(jnp.bfloat16)

def inverse_table():
    times_col = jnp.arange(NT, dtype=jnp.int32)[:, None]
    freq_row = jnp.arange(1, NF + 1, dtype=jnp.int32)[None, :]
    angles = (times_col * freq_row % NT).astype(jnp.float32) * (2.0 * math.pi / NT)
    normalizing_scale = 2.0 / math.sqrt(NT)
    stacked = jnp.stack([jnp.cos(angles) * normalizing_scale, -jnp.sin(angles) * normalizing_scale], axis=2)
    return stacked.reshape(NT, 2 * NF)

def complex_mixing(real_part, imag_part):
    upper = jnp.stack([real_part, -imag_part], axis=1)
    lower = jnp.stack([imag_part, real_part], axis=1)
    return jnp.stack([upper, lower], axis=0)

def reference(records, targets, aperture):
    forward_fourier = forward_table().astype(jnp.float32)
    desired_spectra = jnp.einsum('tsr,tp->srp', targets.astype(jnp.float32), forward_fourier).astype(jnp.bfloat16)
    running = jnp.zeros((NF, 2, NS, R), jnp.float32)
    receivers = jnp.arange(R, dtype=jnp.int32)
    for source_line in range(NL):
        trace_spectra = jnp.einsum('crt,tp->cpr', records[source_line].astype(jnp.float32), forward_fourier)
        trace_spectra = trace_spectra.astype(jnp.bfloat16).reshape(NC, 2, NF, R)
        onehot = (aperture[:, source_line, :, None] == receivers).astype(jnp.float32)
        picked = jnp.einsum('scr,srp->scp', onehot, desired_spectra.astype(jnp.float32))
        mixing = complex_mixing(picked[:, :, :NF], picked[:, :, NF:])
        running = running + jnp.einsum('qspcf,cpfr->fqsr', mixing, trace_spectra.astype(jnp.float32))
    flat_traces = running.reshape(2 * NF, NS * R)
    predicted = jnp.dot(inverse_table(), flat_traces, precision=lax.Precision.HIGHEST, preferred_element_type=jnp.float32)
    return predicted.reshape(NT, NS, R).astype(jnp.bfloat16)
```

```python
import functools
import math

import jax
import jax.numpy as jnp
from jax import lax
from jax.experimental import pallas as pl
from jax.experimental.pallas import tpu as pltpu
from jax.sharding import PartitionSpec as P

NT = 2048
NF = 256
LOW = 32


def fourier_table(bins, start, count):
    blocks = NF // bins
    freq = jnp.arange(1, NF + 1, dtype=jnp.int32).reshape(blocks, 1, bins)
    freq = jnp.broadcast_to(freq, (blocks, 2, bins)).reshape(1, 2 * NF)
    is_imag = jnp.arange(2, dtype=jnp.int32).reshape(1, 2, 1)
    is_imag = jnp.broadcast_to(is_imag, (blocks, 2, bins)).reshape(1, 2 * NF) == 1

    def trig(times):
        angles = (times[:, None] * freq % NT).astype(jnp.float32) * (2.0 * math.pi / NT)
        return jnp.cos(angles), jnp.sin(angles)

    cos_hi, sin_hi = trig(start + jnp.arange(count // LOW, dtype=jnp.int32) * LOW)
    cos_lo, sin_lo = trig(jnp.arange(LOW, dtype=jnp.int32))
    scale = 1.0 / math.sqrt(NT)
    first = jnp.where(is_imag, -sin_hi, cos_hi) * scale
    second = jnp.where(is_imag, -cos_hi, -sin_hi) * scale
    first, second, cos_lo, sin_lo = lax.optimization_barrier((first, second, cos_lo, sin_lo))
    table = first[:, None] * cos_lo[None] + second[:, None] * sin_lo[None]
    return table.reshape(count, 2 * NF).astype(jnp.bfloat16)


def mix_kernel(lines, columns, held, bins, shots, spectra_ref, picked_ref, out_ref):
    gathers = columns * held
    receivers = out_ref.shape[1]
    rows = columns * bins
    depth = columns * 2 * bins
    taken = 2 * shots * gathers
    wide = held * depth

    k = lax.broadcasted_iota(jnp.int32, (taken, wide), 0)
    j = lax.broadcasted_iota(jnp.int32, (taken, wide), 1)
    k_imag, k_shot, k_gather = k // (shots * gathers), k // gathers % shots, k % gathers
    j_held, j_column, j_imag = j // depth, j % depth // (2 * bins), j // bins % 2
    same = k_gather == j_column * held + j_held
    crossed = k_imag != j_imag
    expand = []
    for shot in range(shots):
        for part in range(2):
            hit = same & (k_shot == shot) & (crossed if part else ~crossed)
            value = jnp.where(hit, 1.0, 0.0)
            if part == 0:
                value = jnp.where(j_imag == 1, -value, value)
            expand.append(value.astype(jnp.bfloat16))
    bin_of_row = lax.broadcasted_iota(jnp.int32, (rows, wide), 0) % bins
    bin_of_column = lax.broadcasted_iota(jnp.int32, (rows, wide), 1) % bins
    same_bin = bin_of_row == bin_of_column

    total = jnp.zeros(out_ref.shape, jnp.float32)
    for line in range(lines):
        block = picked_ref[line * rows : (line + 1) * rows, :]
        mixing = [
            jnp.where(
                same_bin, jnp.dot(block, matrix, preferred_element_type=jnp.float32), 0.0
            ).astype(jnp.bfloat16)
            for matrix in expand
        ]
        held_rows = slice(line * depth, (line + 1) * depth)
        spectra = jnp.concatenate(
            [spectra_ref[held_rows, h * receivers : (h + 1) * receivers] for h in range(held)], axis=0
        )
        total += jnp.dot(
            jnp.concatenate(mixing, axis=0), spectra, preferred_element_type=jnp.float32
        )
    out_ref[...] = total.astype(out_ref.dtype)


def spread_kernel(
    lines, columns, gathers, spectra_ref, targets_ref, aperture_ref, table_ref,
    spectra_out, picked_out,
    apertures, traces_here, traces, picked, send, recv, own, line_send, line_recv,
):
    devices = lines * columns
    line = lax.axis_index("xline")
    shot_here = lax.axis_index("shot")
    shots, time_rows, receivers = targets_ref.shape
    width = traces.shape[2]
    me = lax.axis_index("xline") * columns + lax.axis_index("shot")
    mesh_id = pl.DeviceIdType.MESH
    barrier = pltpu.get_barrier_semaphore()

    def greet(step, _):
        peer = lax.rem(me + step, devices)
        pl.semaphore_signal(
            barrier, inc=1,
            device_id={"xline": peer // columns, "shot": lax.rem(peer, columns)},
            device_id_type=mesh_id,
        )
        return 0

    lax.fori_loop(1, devices, greet, 0)
    pl.semaphore_wait(barrier, devices - 1)

    def line_of(step):
        far, other = step // columns // 2, lax.rem(step // columns, 2)
        moved = lax.rem(line + far * (lines // 2), lines)
        return moved + other * (1 - 2 * lax.rem(moved, 2))

    def copy_of(which, source, target, step):
        peer = line_of(step) * columns + lax.rem(shot_here + step, columns)
        return pltpu.make_async_remote_copy(
            src_ref=source.at[peer],
            dst_ref=target.at[me],
            send_sem=send.at[which, step],
            recv_sem=recv.at[which, step],
            device_id={"xline": peer // columns, "shot": lax.rem(peer, columns)},
            device_id_type=mesh_id,
        )

    def arrival_of(which, target, step):
        origin = line_of(step) * columns + lax.rem(shot_here + devices - step, columns)
        return pltpu.make_async_remote_copy(
            src_ref=target.at[origin],
            dst_ref=target.at[origin],
            send_sem=send.at[which, step],
            recv_sem=recv.at[which, step],
            device_id={"xline": origin // columns, "shot": lax.rem(origin, columns)},
            device_id_type=mesh_id,
        )

    def along_line(which, source, target, step):
        peer = lax.rem(line + step, lines)
        return pltpu.make_async_remote_copy(
            src_ref=source.at[peer] if which else source,
            dst_ref=target.at[line],
            send_sem=line_send.at[which, step],
            recv_sem=line_recv.at[which, step],
            device_id={"xline": peer},
            device_id_type=mesh_id,
        )

    def from_line(which, target, step):
        origin = lax.rem(line + lines - step, lines)
        return pltpu.make_async_remote_copy(
            src_ref=target.at[origin],
            dst_ref=target.at[origin],
            send_sem=line_send.at[which, step],
            recv_sem=line_recv.at[which, step],
            device_id={"xline": origin},
            device_id_type=mesh_id,
        )

    def begin(step, _):
        copy_of(0, spectra_ref, spectra_out, step).start()
        return 0

    for step in range(1, lines):
        along_line(0, aperture_ref, apertures, step).start()
    lax.fori_loop(1, 2 * columns, begin, 0)
    mine = [
        pltpu.make_async_copy(aperture_ref, apertures.at[line], own.at[0]),
        pltpu.make_async_copy(spectra_ref.at[me], spectra_out.at[me], own.at[1]),
    ]
    for copy in mine:
        copy.start()
    for copy in mine:
        copy.wait()
    for step in range(1, lines):
        from_line(0, apertures, step).wait_recv()

    wanted = []
    for l in range(lines):
        wanted += [apertures[l, s : s + 1, :] for s in range(shots)]
        if width > shots * gathers:
            wanted.append(jnp.zeros((1, width - shots * gathers), jnp.int32))
    wanted = jnp.concatenate(wanted, axis=1)
    lane = lax.broadcasted_iota(jnp.int32, (receivers, lines * width), 1)
    receiver = lax.broadcasted_iota(jnp.int32, (receivers, lines * width), 0)
    total = jnp.zeros((time_rows, lines * width), jnp.float32)
    for shot in range(shots):
        hit = (lane % width // gathers == shot) & (receiver == wanted)
        onehot = jnp.where(hit, 1.0, 0.0).astype(jnp.bfloat16)
        total += jnp.dot(targets_ref[shot], onehot, preferred_element_type=jnp.float32)
    total = total.astype(jnp.bfloat16)
    for l in range(lines):
        traces_here[l] = total[:, l * width : (l + 1) * width]

    arrival_of(0, spectra_out, 1).wait_recv()
    for step in range(1, lines):
        along_line(1, traces_here, traces, step).start()
    lax.fori_loop(2 * columns, devices, begin, 0)
    keep = pltpu.make_async_copy(traces_here.at[line], traces.at[line], own.at[2])
    keep.start()
    keep.wait()
    for step in range(1, lines):
        from_line(1, traces, step).wait_recv()

    value = jnp.zeros((table_ref.shape[1], width), jnp.float32)
    for l in range(lines):
        value += lax.dot_general(
            table_ref[l * time_rows : (l + 1) * time_rows, :], traces[l],
            (((0,), (0,)), ((), ())),
            preferred_element_type=jnp.float32,
        )
    picked[...] = value.astype(jnp.bfloat16).reshape(picked.shape)
    arrival_of(0, spectra_out, 2).wait_recv()

    def begin_picked(step, _):
        copy_of(1, picked, picked_out, step).start()
        return 0

    lax.fori_loop(1, devices, begin_picked, 0)
    keep = pltpu.make_async_copy(picked.at[me], picked_out.at[me], own.at[3])
    keep.start()
    keep.wait()
    for step in range(1, lines):
        along_line(0, aperture_ref, apertures, step).wait_send()
        along_line(1, traces_here, traces, step).wait_send()

    def finish(step, _):
        copy_of(0, spectra_ref, spectra_out, step).wait_send()
        copy_of(1, picked, picked_out, step).wait_send()
        arrival_of(1, picked_out, step).wait_recv()
        return 0

    def arrived(step, _):
        arrival_of(0, spectra_out, step).wait_recv()
        return 0

    lax.fori_loop(3, devices, arrived, 0)
    lax.fori_loop(1, devices, finish, 0)


def collect_kernel(lines, columns, running_ref, out_ref, send, recv, own):
    line = lax.axis_index("xline")
    me = lax.axis_index("shot")
    core_line = line + 1 - 2 * lax.rem(line, 2)
    far_line = lax.rem(line + lines // 2, lines)
    diagonal_line = lax.rem(core_line + lines // 2, lines)
    mesh_id = pl.DeviceIdType.MESH
    barrier = pltpu.get_barrier_semaphore()

    def greet(step, _):
        pl.semaphore_signal(
            barrier, inc=1, device_id={"shot": lax.rem(me + step, columns)}, device_id_type=mesh_id
        )
        return 0

    lax.fori_loop(1, columns, greet, 0)
    for peer in (core_line, far_line):
        pl.semaphore_signal(barrier, inc=1, device_id={"xline": peer}, device_id_type=mesh_id)
    pl.semaphore_wait(barrier, columns + 1)

    def across(step):
        peer = lax.rem(me + step, columns)
        return pltpu.make_async_remote_copy(
            src_ref=running_ref.at[peer],
            dst_ref=out_ref.at[line * columns + me],
            send_sem=send.at[0, step],
            recv_sem=recv.at[0, step],
            device_id={"shot": peer},
            device_id_type=mesh_id,
        )

    def onward(stage, source_line, peer_line, step):
        slot = source_line * columns + lax.rem(me + columns - step, columns)
        return pltpu.make_async_remote_copy(
            src_ref=out_ref.at[slot],
            dst_ref=out_ref.at[slot],
            send_sem=send.at[stage, step],
            recv_sem=recv.at[stage, step],
            device_id={"xline": peer_line},
            device_id_type=mesh_id,
        )

    def begin(step, _):
        across(step).start()
        return 0

    lax.fori_loop(1, columns, begin, 0)
    mine = pltpu.make_async_copy(running_ref.at[me], out_ref.at[line * columns + me], own.at[0])
    mine.start()
    mine.wait()
    onward(2, line, far_line, 0).start()
    onward(1, line, core_line, 0).start()

    def relay(step, _):
        slot = line * columns + lax.rem(me + columns - step, columns)
        pltpu.make_async_remote_copy(
            src_ref=out_ref.at[slot],
            dst_ref=out_ref.at[slot],
            send_sem=send.at[0, step],
            recv_sem=recv.at[0, step],
            device_id={"shot": lax.rem(me + columns - step, columns)},
            device_id_type=mesh_id,
        ).wait_recv()
        onward(2, line, far_line, step).start()
        onward(1, line, core_line, step).start()
        return 0

    lax.fori_loop(1, columns, relay, 0)

    def turn(step, _):
        onward(2, far_line, far_line, step).wait_recv()
        onward(3, far_line, core_line, step).start()
        return 0

    lax.fori_loop(0, columns, turn, 0)

    def finish(step, _):
        onward(1, core_line, core_line, step).wait_recv()
        onward(3, diagonal_line, core_line, step).wait_recv()
        onward(1, line, core_line, step).wait_send()
        onward(2, line, far_line, step).wait_send()
        onward(3, far_line, core_line, step).wait_send()
        return 0

    lax.fori_loop(0, columns, finish, 0)

    def sent(step, _):
        across(step).wait_send()
        return 0

    lax.fori_loop(1, columns, sent, 0)


def xor_of(index, step):
    result, weight = 0, 1
    while weight < 64:
        bit = lax.rem(index // weight + step // weight, 2)
        result, weight = result + bit * weight, weight * 2
    return result


def fused_kernel(
    lines, columns, bins, low,
    records_ref, targets_ref, aperture_ref, out_ref,
    records, table, inverse, expand, mixing, apertures, traces_here, traces,
    sent, spectra, picked_here, picked, running, gathered,
    load, own, near_send, near_recv, wide_send, wide_recv, run_send, run_recv,
):
    f32, bf16 = jnp.float32, jnp.bfloat16
    devices = lines * columns
    halves = records.shape[0]
    shots, time_rows, receivers = targets_ref.shape
    held = records_ref.shape[0] // receivers
    part = receivers // halves
    gathers = aperture_ref.shape[1]
    chosen = shots * gathers
    width = 2 * chosen
    rows = columns * bins
    depth = 2 * bins
    line = lax.axis_index("xline")
    shot_here = lax.axis_index("shot")
    me = line * columns + shot_here
    mesh_id = pl.DeviceIdType.MESH
    barrier = pltpu.get_barrier_semaphore()

    def greet(step, _):
        peer = lax.rem(me + step, devices)
        pl.semaphore_signal(
            barrier, inc=1,
            device_id={"xline": peer // columns, "shot": lax.rem(peer, columns)},
            device_id_type=mesh_id,
        )
        return 0

    lax.fori_loop(1, devices, greet, 0)

    loads = []
    for h in range(halves):
        for g in range(held):
            loads.append(
                pltpu.make_async_copy(
                    records_ref.at[pl.ds(g * receivers + h * part, part), :],
                    records.at[h, pl.ds(g * part, part), :],
                    load.at[h, g],
                )
            )
    for copy in loads:
        copy.start()

    group = 4 * depth // 2
    scale = 1.0 / math.sqrt(NT)
    step_angle = 2.0 * math.pi / NT
    row = lax.broadcasted_iota(jnp.int32, (group, 128), 0)
    lane = lax.broadcasted_iota(jnp.int32, (group, 128), 1)
    freq = row // depth * bins + row % bins + 1
    turn = (row // bins % 2) * (NT // 4)
    group_bins = group // depth * bins

    def wave(first_freq, first_time):
        angle = ((freq + first_freq) * (lane + first_time) + turn) % NT
        return jnp.cos(angle.astype(f32) * step_angle) * scale

    across_time = 2.0 * jnp.cos((freq * 128 % NT).astype(f32) * step_angle)
    across_rows = 2.0 * jnp.cos((lane * group_bins % NT).astype(f32) * step_angle)
    flip = (1 - 2 * (freq % 2)).astype(f32)

    def fill(block, carry):
        at0, next0, at1, next1 = carry
        here = pl.ds(pl.multiple_of(block * group, group), group)
        now, later = at0, at1
        for k in range(NT // 256):
            table[here, k * 128 : (k + 1) * 128] = now.astype(bf16)
            table[here, NT // 2 + k * 128 : NT // 2 + (k + 1) * 128] = (now * flip).astype(bf16)
            now, later = later, across_time * later - now
        return next0, across_rows * next0 - at0, next1, across_rows * next1 - at1

    lax.fori_loop(
        0, 2 * NF // group, fill,
        (wave(0, 0), wave(group_bins, 0), wave(0, 128), wave(group_bins, 128)),
    )

    def transform(h):
        for g in range(held):
            loads[h * held + g].wait()
        value = lax.dot_general(
            table[...], records[h], (((1,), (1,)), ((), ())), preferred_element_type=f32
        )
        sent[h] = value.astype(bf16).reshape(sent.shape[1:])

    def wide(which, source, target, step):
        far, near = step // 8, lax.rem(step, 8)
        line_step = near // 4 * 2 + lax.rem(near, 2)
        shot_step = far * 2 + lax.rem(near // 2, 2)
        peer_line, peer_shot = xor_of(line, line_step), xor_of(shot_here, shot_step)
        return pltpu.make_async_remote_copy(
            src_ref=source.at[peer_line * columns + peer_shot],
            dst_ref=target.at[me],
            send_sem=wide_send.at[which, step],
            recv_sem=wide_recv.at[which, step],
            device_id={"xline": peer_line, "shot": peer_shot},
            device_id_type=mesh_id,
        )

    def wide_copy(which, step):
        if which < halves:
            return wide(which, sent.at[which], spectra.at[which], step)
        return wide(which, picked_here, picked, step)

    def start_wide(which, first, last):
        def begin(j, _):
            wide_copy(which, devices - 1 - j).start()
            return 0

        lax.fori_loop(first, last, begin, 0)

    def wait_wide(which):
        def finish(j, _):
            wide_copy(which, devices - 1 - j).wait()
            return 0

        lax.fori_loop(0, devices - 1, finish, 0)

    def along_line(which, step):
        peer = xor_of(line, step)
        source = traces_here.at[peer] if which else aperture_ref
        target = traces if which else apertures
        return pltpu.make_async_remote_copy(
            src_ref=source,
            dst_ref=target.at[line],
            send_sem=near_send.at[which, step],
            recv_sem=near_recv.at[which, step],
            device_id={"xline": peer},
            device_id_type=mesh_id,
        )

    transform(0)
    pl.semaphore_wait(barrier, devices - 1)
    for step in range(1, lines):
        along_line(0, step).start()
    start_wide(0, 0, devices - 1)
    mine = [
        pltpu.make_async_copy(aperture_ref, apertures.at[line], own.at[0]),
        pltpu.make_async_copy(sent.at[0, me], spectra.at[0, me], own.at[1]),
    ]
    for copy in mine:
        copy.start()
    transform(1)
    keep_one = pltpu.make_async_copy(sent.at[1, me], spectra.at[1, me], own.at[2])
    keep_one.start()
    for copy in mine:
        copy.wait()
    for step in range(1, lines):
        along_line(0, step).wait()

    wanted = []
    for l in range(lines):
        wanted += [apertures[l, s : s + 1, :] for s in range(shots)] * 2
    wanted = jnp.concatenate(wanted, axis=1)
    lane = lax.broadcasted_iota(jnp.int32, (receivers, lines * width), 1)
    receiver = lax.broadcasted_iota(jnp.int32, (receivers, lines * width), 0)
    total = jnp.zeros((time_rows, lines * width), f32)
    for shot in range(shots):
        hit = (lane % chosen // gathers == shot) & (receiver == wanted)
        onehot = jnp.where(hit, 1.0, 0.0).astype(bf16)
        total += jnp.dot(targets_ref[shot], onehot, preferred_element_type=f32)
    fold = time_rows // 2
    lane = lax.broadcasted_iota(jnp.int32, (fold, lines * width), 1)
    folded = jnp.where(lane % width < chosen, total[:fold], total[fold:]).astype(bf16)
    for l in range(lines):
        traces_here[l] = folded[:, l * width : (l + 1) * width]
    for step in range(1, lines):
        along_line(1, step).start()
    keep = pltpu.make_async_copy(traces_here.at[line], traces.at[line], own.at[3])
    keep.start()
    start_wide(1, 0, low)

    taken = width
    across = held * columns * depth
    for shot in range(shots):
        for q in range(2):
            k = lax.broadcasted_iota(jnp.int32, (taken, held * columns * depth), 0)
            j = lax.broadcasted_iota(jnp.int32, (taken, held * columns * depth), 1)
            k_imag, k_shot, k_gather = k // chosen, k // gathers % shots, k % gathers
            j_held, j_column, j_imag = j // (columns * depth), j // depth % columns, j // bins % 2
            hit = (k_gather == j_column * held + j_held) & (k_shot == shot)
            hit = hit & ((k_imag != j_imag) if q else (k_imag == j_imag))
            value = jnp.where(hit, 1.0, 0.0)
            if q == 0:
                value = jnp.where(j_imag == 1, -value, value)
            expand[shot * 2 + q] = value.astype(bf16)
    slab = line * time_rows
    for c in range(time_rows // 128):
        block = table[:, pl.ds(pl.multiple_of(slab + c * 128, 128), 128)].astype(f32)
        inverse[c * 128 : (c + 1) * 128, :] = (block * 2.0).T.astype(bf16)

    keep.wait()
    for step in range(1, lines):
        along_line(1, step).wait()
    ahead = jnp.zeros((2 * NF, width), f32)
    behind = jnp.zeros((2 * NF, width), f32)
    for l in range(lines):
        base = l * time_rows
        ahead += jnp.dot(table[:, base : base + fold], traces[l], preferred_element_type=f32)
        behind += jnp.dot(
            table[:, base + fold : base + time_rows], traces[l], preferred_element_type=f32
        )
    real = (ahead + pltpu.roll(behind, chosen, 1)).reshape(devices, depth, width)[:, :bins]
    imag = (pltpu.roll(ahead, chosen, 1) + behind).reshape(devices, depth, width)[:, bins:]
    lane = lax.broadcasted_iota(jnp.int32, (devices, bins, width), 2)
    picked_here[...] = jnp.where(lane < chosen, real, imag).astype(bf16)
    start_wide(2, 0, devices - 1)
    start_wide(1, low, devices - 1)
    keep = pltpu.make_async_copy(picked_here.at[me], picked.at[me], own.at[4])
    keep.start()

    wait_wide(0)
    keep.wait()
    wait_wide(2)

    same_bin = (
        lax.broadcasted_iota(jnp.int32, (rows, across), 0) % bins
        == lax.broadcasted_iota(jnp.int32, (rows, across), 1) % bins
    )
    span = columns * depth
    for l in range(lines):
        block = picked[l * columns : (l + 1) * columns].astype(f32).reshape(rows, width).astype(bf16)
        for sq in range(2 * shots):
            value = jnp.dot(block, expand[sq], preferred_element_type=f32)
            value = jnp.where(same_bin, value, 0.0).astype(bf16)
            for g in range(held):
                first = (g * lines + l) * span
                mixing[sq * rows : (sq + 1) * rows, first : first + span] = (
                    value[:, g * span : (g + 1) * span]
                )

    def hop(h, stage, source_line, peer_line, step):
        slot = source_line * columns + xor_of(shot_here, step)
        return pltpu.make_async_remote_copy(
            src_ref=gathered.at[h, slot],
            dst_ref=gathered.at[h, slot],
            send_sem=run_send.at[h, stage, step],
            recv_sem=run_recv.at[h, stage, step],
            device_id={"xline": peer_line},
            device_id_type=mesh_id,
        )

    def spread(h, step):
        peer = xor_of(shot_here, step)
        return pltpu.make_async_remote_copy(
            src_ref=running.at[h, peer],
            dst_ref=gathered.at[h, me],
            send_sem=run_send.at[h, 0, step],
            recv_sem=run_recv.at[h, 0, step],
            device_id={"shot": peer},
            device_id_type=mesh_id,
        )

    core_line = xor_of(line, 1)
    far_line = xor_of(line, 2)
    diagonal_line = xor_of(line, 3)

    def mix(h):
        total = jnp.zeros((2 * shots * rows, part), f32)
        for g in range(held):
            block = spectra[h, :, :, g * part : (g + 1) * part].reshape(2 * NF, part)
            total += jnp.dot(
                mixing[:, g * 2 * NF : (g + 1) * 2 * NF], block, preferred_element_type=f32
            )
        for column in range(columns):
            for shot in range(shots):
                pieces = [
                    total[(shot * 2 + q) * rows + column * bins :][:bins] for q in range(2)
                ]
                running[h, column, shot] = jnp.concatenate(pieces, axis=0).astype(bf16)

        def begin(j, _):
            spread(h, columns - 1 - j).start()
            return 0

        lax.fori_loop(0, columns - 1, begin, 0)
        keep = pltpu.make_async_copy(running.at[h, shot_here], gathered.at[h, me], own.at[5 + h])
        keep.start()
        keep.wait()
        hop(h, 2, line, far_line, 0).start()
        hop(h, 1, line, core_line, 0).start()

    def relay(h):
        def pass_on(j, _):
            step = j + 1
            spread(h, step).wait()
            hop(h, 2, line, far_line, step).start()
            hop(h, 1, line, core_line, step).start()
            return 0

        lax.fori_loop(0, columns - 1, pass_on, 0)

    def turn_over(h):
        def pass_on(step, _):
            hop(h, 2, far_line, far_line, step).wait_recv()
            hop(h, 3, far_line, core_line, step).start()
            return 0

        lax.fori_loop(0, columns, pass_on, 0)

    def complete(h):
        def finish(step, _):
            hop(h, 1, core_line, core_line, step).wait_recv()
            hop(h, 3, diagonal_line, core_line, step).wait_recv()
            hop(h, 1, line, core_line, step).wait_send()
            hop(h, 2, line, far_line, step).wait_send()
            hop(h, 3, far_line, core_line, step).wait_send()
            return 0

        lax.fori_loop(0, columns, finish, 0)

    def invert(h):
        for shot in range(shots):
            block = gathered[h, :, shot].reshape(2 * NF, part)
            out_ref[shot, :, h * part : (h + 1) * part] = jnp.dot(
                inverse[...], block, preferred_element_type=f32
            ).astype(bf16)

    mix(0)
    keep_one.wait()
    wait_wide(1)
    mix(1)
    relay(0)
    turn_over(0)
    relay(1)
    complete(0)
    invert(0)
    turn_over(1)
    complete(1)
    invert(1)


def fused(records, targets, aperture):
    bf16 = jnp.bfloat16
    lines = lax.axis_size("xline")
    columns = lax.axis_size("shot")
    devices = lines * columns
    bins = NF // devices
    time_rows, shots, receivers = targets.shape
    held = records.shape[1]
    gathers = aperture.shape[2]
    halves, part = 2, receivers // 2
    width = 2 * shots * gathers
    wide = held * columns * 2 * bins
    in_vmem = pl.BlockSpec(memory_space=pltpu.VMEM)
    dma = pltpu.SemaphoreType.DMA
    vmem = lambda *shape: pltpu.VMEM(shape, bf16)
    out = pl.pallas_call(
        functools.partial(fused_kernel, lines, columns, bins, 10),
        out_shape=jax.ShapeDtypeStruct((shots, time_rows, receivers), bf16),
        in_specs=[pl.BlockSpec(memory_space=pl.ANY), in_vmem, in_vmem],
        out_specs=in_vmem,
        scratch_shapes=[
            vmem(halves, held * part, NT),
            vmem(2 * NF, NT),
            vmem(time_rows, 2 * NF),
            vmem(2 * shots, width, wide),
            vmem(2 * shots * columns * bins, lines * wide),
            pltpu.VMEM((lines, shots, gathers), jnp.int32),
            vmem(lines, time_rows // 2, width),
            vmem(lines, time_rows // 2, width),
            vmem(halves, devices, 2 * bins, held * part),
            vmem(halves, devices, 2 * bins, held * part),
            vmem(devices, bins, width),
            vmem(devices, bins, width),
            vmem(halves, columns, shots, 2 * bins, part),
            vmem(halves, devices, shots, 2 * bins, part),
            dma((halves, held)), dma((7,)), dma((2, lines)), dma((2, lines)),
            dma((3, devices)), dma((3, devices)),
            dma((halves, 4, columns)), dma((halves, 4, columns)),
        ],
        compiler_params=pltpu.CompilerParams(collective_id=2, has_side_effects=True),
    )(records.reshape(held * receivers, NT), targets.transpose(1, 0, 2), aperture.reshape(shots, gathers))
    return out.transpose(1, 0, 2)


def on_device(records, targets, aperture):
    f32, bf16 = jnp.float32, jnp.bfloat16
    lines = lax.axis_size("xline")
    columns = lax.axis_size("shot")
    devices = lines * columns
    bins = NF // devices
    time_rows, shots, receivers = targets.shape
    held = records.shape[1]
    gathers = aperture.shape[2]
    if (lines, columns, bins, 2 * shots * gathers, receivers) == (4, 8, 8, 128, 256):
        return fused(records, targets, aperture)
    table = fourier_table(bins, 0, NT)
    chosen = shots * gathers
    padded = -(-chosen // 128) * 128

    spectra = jnp.einsum(
        "tp,kt->pk", table, records.reshape(held * receivers, NT), preferred_element_type=f32
    ).astype(bf16)

    spectra = spectra.reshape(devices, 2 * bins, held * receivers)
    in_vmem = pl.BlockSpec(memory_space=pltpu.VMEM)
    dma = pltpu.SemaphoreType.DMA
    spectra, picked = pl.pallas_call(
        functools.partial(spread_kernel, lines, columns, gathers),
        out_shape=[
            jax.ShapeDtypeStruct(spectra.shape, bf16),
            jax.ShapeDtypeStruct((devices, 2 * bins, padded), bf16),
        ],
        in_specs=[in_vmem] * 4,
        out_specs=[in_vmem] * 2,
        scratch_shapes=[
            pltpu.VMEM((lines, shots, gathers), jnp.int32),
            pltpu.VMEM((lines, time_rows, padded), bf16),
            pltpu.VMEM((lines, time_rows, padded), bf16),
            pltpu.VMEM((devices, 2 * bins, padded), bf16),
            dma((2, devices)), dma((2, devices)), dma((4,)), dma((2, lines)), dma((2, lines)),
        ],
        compiler_params=pltpu.CompilerParams(collective_id=0, has_side_effects=True),
    )(spectra, targets.transpose(1, 0, 2), aperture.reshape(shots, gathers), table)
    picked = picked.reshape(devices, 2, bins, padded)[..., :chosen]
    picked = jnp.concatenate([picked[:, 0], picked[:, 1]], axis=-1)

    running = pl.pallas_call(
        functools.partial(mix_kernel, lines, columns, held, bins, shots),
        out_shape=jax.ShapeDtypeStruct((shots * 2 * columns * bins, receivers), bf16),
        in_specs=[pl.BlockSpec(memory_space=pltpu.VMEM)] * 2,
        out_specs=pl.BlockSpec(memory_space=pltpu.VMEM),
    )(spectra.reshape(2 * NF, held * receivers), picked.reshape(NF, -1))
    running = running.reshape(shots, 2, columns, bins, receivers).transpose(2, 0, 1, 3, 4)
    running = running.reshape(columns, shots, 2 * bins, receivers)
    running = pl.pallas_call(
        functools.partial(collect_kernel, lines, columns),
        out_shape=jax.ShapeDtypeStruct((devices, *running.shape[1:]), bf16),
        in_specs=[in_vmem],
        out_specs=in_vmem,
        scratch_shapes=[dma((4, columns)), dma((4, columns)), dma((1,))],
        compiler_params=pltpu.CompilerParams(collective_id=1, has_side_effects=True),
    )(running)
    running = running.transpose(0, 2, 1, 3).reshape(2 * NF, shots, receivers)

    rows = fourier_table(bins, lax.axis_index("xline") * time_rows, time_rows)
    out = jnp.einsum("tp,psr->tsr", rows * 2, running, preferred_element_type=f32)
    return out.astype(bf16)


def solution(mesh):
    in_specs = (P("xline", "shot", None, None), P("xline", "shot", None), P("shot", "xline", None))
    out_specs = P("xline", "shot", None)
    return jax.shard_map(
        on_device, mesh=mesh, in_specs=in_specs, out_specs=out_specs, check_vma=False
    )
```

```python
import functools
import math

import jax
import jax.numpy as jnp
from jax import lax
from jax.experimental import pallas as pl
from jax.experimental.pallas import tpu as pltpu
from jax.sharding import PartitionSpec as P

NT = 2048
NF = 256
LOW = 32


def fourier_table(bins, start, count):
    blocks = NF // bins
    freq = jnp.arange(1, NF + 1, dtype=jnp.int32).reshape(blocks, 1, bins)
    freq = jnp.broadcast_to(freq, (blocks, 2, bins)).reshape(1, 2 * NF)
    is_imag = jnp.arange(2, dtype=jnp.int32).reshape(1, 2, 1)
    is_imag = jnp.broadcast_to(is_imag, (blocks, 2, bins)).reshape(1, 2 * NF) == 1

    def trig(times):
        angles = (times[:, None] * freq % NT).astype(jnp.float32) * (2.0 * math.pi / NT)
        return jnp.cos(angles), jnp.sin(angles)

    cos_hi, sin_hi = trig(start + jnp.arange(count // LOW, dtype=jnp.int32) * LOW)
    cos_lo, sin_lo = trig(jnp.arange(LOW, dtype=jnp.int32))
    scale = 1.0 / math.sqrt(NT)
    first = jnp.where(is_imag, -sin_hi, cos_hi) * scale
    second = jnp.where(is_imag, -cos_hi, -sin_hi) * scale
    first, second, cos_lo, sin_lo = lax.optimization_barrier((first, second, cos_lo, sin_lo))
    table = first[:, None] * cos_lo[None] + second[:, None] * sin_lo[None]
    return table.reshape(count, 2 * NF).astype(jnp.bfloat16)


def mix_kernel(lines, columns, held, bins, shots, spectra_ref, picked_ref, out_ref):
    gathers = columns * held
    receivers = out_ref.shape[1]
    rows = columns * bins
    depth = columns * 2 * bins
    taken = 2 * shots * gathers
    wide = held * depth

    k = lax.broadcasted_iota(jnp.int32, (taken, wide), 0)
    j = lax.broadcasted_iota(jnp.int32, (taken, wide), 1)
    k_imag, k_shot, k_gather = k // (shots * gathers), k // gathers % shots, k % gathers
    j_held, j_column, j_imag = j // depth, j % depth // (2 * bins), j // bins % 2
    same = k_gather == j_column * held + j_held
    crossed = k_imag != j_imag
    expand = []
    for shot in range(shots):
        for part in range(2):
            hit = same & (k_shot == shot) & (crossed if part else ~crossed)
            value = jnp.where(hit, 1.0, 0.0)
            if part == 0:
                value = jnp.where(j_imag == 1, -value, value)
            expand.append(value.astype(jnp.bfloat16))
    bin_of_row = lax.broadcasted_iota(jnp.int32, (rows, wide), 0) % bins
    bin_of_column = lax.broadcasted_iota(jnp.int32, (rows, wide), 1) % bins
    same_bin = bin_of_row == bin_of_column

    total = jnp.zeros(out_ref.shape, jnp.float32)
    for line in range(lines):
        block = picked_ref[line * rows : (line + 1) * rows, :]
        mixing = [
            jnp.where(
                same_bin, jnp.dot(block, matrix, preferred_element_type=jnp.float32), 0.0
            ).astype(jnp.bfloat16)
            for matrix in expand
        ]
        held_rows = slice(line * depth, (line + 1) * depth)
        spectra = jnp.concatenate(
            [spectra_ref[held_rows, h * receivers : (h + 1) * receivers] for h in range(held)], axis=0
        )
        total += jnp.dot(
            jnp.concatenate(mixing, axis=0), spectra, preferred_element_type=jnp.float32
        )
    out_ref[...] = total.astype(out_ref.dtype)


def spread_kernel(
    lines, columns, gathers, spectra_ref, targets_ref, aperture_ref, table_ref,
    spectra_out, picked_out,
    apertures, traces_here, traces, picked, send, recv, own, line_send, line_recv,
):
    devices = lines * columns
    line = lax.axis_index("xline")
    shot_here = lax.axis_index("shot")
    shots, time_rows, receivers = targets_ref.shape
    width = traces.shape[2]
    me = lax.axis_index("xline") * columns + lax.axis_index("shot")
    mesh_id = pl.DeviceIdType.MESH
    barrier = pltpu.get_barrier_semaphore()

    def greet(step, _):
        peer = lax.rem(me + step, devices)
        pl.semaphore_signal(
            barrier, inc=1,
            device_id={"xline": peer // columns, "shot": lax.rem(peer, columns)},
            device_id_type=mesh_id,
        )
        return 0

    lax.fori_loop(1, devices, greet, 0)
    pl.semaphore_wait(barrier, devices - 1)

    def line_of(step):
        far, other = step // columns // 2, lax.rem(step // columns, 2)
        moved = lax.rem(line + far * (lines // 2), lines)
        return moved + other * (1 - 2 * lax.rem(moved, 2))

    def copy_of(which, source, target, step):
        peer = line_of(step) * columns + lax.rem(shot_here + step, columns)
        return pltpu.make_async_remote_copy(
            src_ref=source.at[peer],
            dst_ref=target.at[me],
            send_sem=send.at[which, step],
            recv_sem=recv.at[which, step],
            device_id={"xline": peer // columns, "shot": lax.rem(peer, columns)},
            device_id_type=mesh_id,
        )

    def arrival_of(which, target, step):
        origin = line_of(step) * columns + lax.rem(shot_here + devices - step, columns)
        return pltpu.make_async_remote_copy(
            src_ref=target.at[origin],
            dst_ref=target.at[origin],
            send_sem=send.at[which, step],
            recv_sem=recv.at[which, step],
            device_id={"xline": origin // columns, "shot": lax.rem(origin, columns)},
            device_id_type=mesh_id,
        )

    def along_line(which, source, target, step):
        peer = lax.rem(line + step, lines)
        return pltpu.make_async_remote_copy(
            src_ref=source.at[peer] if which else source,
            dst_ref=target.at[line],
            send_sem=line_send.at[which, step],
            recv_sem=line_recv.at[which, step],
            device_id={"xline": peer},
            device_id_type=mesh_id,
        )

    def from_line(which, target, step):
        origin = lax.rem(line + lines - step, lines)
        return pltpu.make_async_remote_copy(
            src_ref=target.at[origin],
            dst_ref=target.at[origin],
            send_sem=line_send.at[which, step],
            recv_sem=line_recv.at[which, step],
            device_id={"xline": origin},
            device_id_type=mesh_id,
        )

    def begin(step, _):
        copy_of(0, spectra_ref, spectra_out, step).start()
        return 0

    for step in range(1, lines):
        along_line(0, aperture_ref, apertures, step).start()
    lax.fori_loop(1, 2 * columns, begin, 0)
    mine = [
        pltpu.make_async_copy(aperture_ref, apertures.at[line], own.at[0]),
        pltpu.make_async_copy(spectra_ref.at[me], spectra_out.at[me], own.at[1]),
    ]
    for copy in mine:
        copy.start()
    for copy in mine:
        copy.wait()
    for step in range(1, lines):
        from_line(0, apertures, step).wait_recv()

    wanted = []
    for l in range(lines):
        wanted += [apertures[l, s : s + 1, :] for s in range(shots)]
        if width > shots * gathers:
            wanted.append(jnp.zeros((1, width - shots * gathers), jnp.int32))
    wanted = jnp.concatenate(wanted, axis=1)
    lane = lax.broadcasted_iota(jnp.int32, (receivers, lines * width), 1)
    receiver = lax.broadcasted_iota(jnp.int32, (receivers, lines * width), 0)
    total = jnp.zeros((time_rows, lines * width), jnp.float32)
    for shot in range(shots):
        hit = (lane % width // gathers == shot) & (receiver == wanted)
        onehot = jnp.where(hit, 1.0, 0.0).astype(jnp.bfloat16)
        total += jnp.dot(targets_ref[shot], onehot, preferred_element_type=jnp.float32)
    total = total.astype(jnp.bfloat16)
    for l in range(lines):
        traces_here[l] = total[:, l * width : (l + 1) * width]

    arrival_of(0, spectra_out, 1).wait_recv()
    for step in range(1, lines):
        along_line(1, traces_here, traces, step).start()
    lax.fori_loop(2 * columns, devices, begin, 0)
    keep = pltpu.make_async_copy(traces_here.at[line], traces.at[line], own.at[2])
    keep.start()
    keep.wait()
    for step in range(1, lines):
        from_line(1, traces, step).wait_recv()

    value = jnp.zeros((table_ref.shape[1], width), jnp.float32)
    for l in range(lines):
        value += lax.dot_general(
            table_ref[l * time_rows : (l + 1) * time_rows, :], traces[l],
            (((0,), (0,)), ((), ())),
            preferred_element_type=jnp.float32,
        )
    picked[...] = value.astype(jnp.bfloat16).reshape(picked.shape)
    arrival_of(0, spectra_out, 2).wait_recv()

    def begin_picked(step, _):
        copy_of(1, picked, picked_out, step).start()
        return 0

    lax.fori_loop(1, devices, begin_picked, 0)
    keep = pltpu.make_async_copy(picked.at[me], picked_out.at[me], own.at[3])
    keep.start()
    keep.wait()
    for step in range(1, lines):
        along_line(0, aperture_ref, apertures, step).wait_send()
        along_line(1, traces_here, traces, step).wait_send()

    def finish(step, _):
        copy_of(0, spectra_ref, spectra_out, step).wait_send()
        copy_of(1, picked, picked_out, step).wait_send()
        arrival_of(1, picked_out, step).wait_recv()
        return 0

    def arrived(step, _):
        arrival_of(0, spectra_out, step).wait_recv()
        return 0

    lax.fori_loop(3, devices, arrived, 0)
    lax.fori_loop(1, devices, finish, 0)


def collect_kernel(lines, columns, running_ref, out_ref, send, recv, own):
    line = lax.axis_index("xline")
    me = lax.axis_index("shot")
    core_line = line + 1 - 2 * lax.rem(line, 2)
    far_line = lax.rem(line + lines // 2, lines)
    diagonal_line = lax.rem(core_line + lines // 2, lines)
    mesh_id = pl.DeviceIdType.MESH
    barrier = pltpu.get_barrier_semaphore()

    def greet(step, _):
        pl.semaphore_signal(
            barrier, inc=1, device_id={"shot": lax.rem(me + step, columns)}, device_id_type=mesh_id
        )
        return 0

    lax.fori_loop(1, columns, greet, 0)
    for peer in (core_line, far_line):
        pl.semaphore_signal(barrier, inc=1, device_id={"xline": peer}, device_id_type=mesh_id)
    pl.semaphore_wait(barrier, columns + 1)

    def across(step):
        peer = lax.rem(me + step, columns)
        return pltpu.make_async_remote_copy(
            src_ref=running_ref.at[peer],
            dst_ref=out_ref.at[line * columns + me],
            send_sem=send.at[0, step],
            recv_sem=recv.at[0, step],
            device_id={"shot": peer},
            device_id_type=mesh_id,
        )

    def onward(stage, source_line, peer_line, step):
        slot = source_line * columns + lax.rem(me + columns - step, columns)
        return pltpu.make_async_remote_copy(
            src_ref=out_ref.at[slot],
            dst_ref=out_ref.at[slot],
            send_sem=send.at[stage, step],
            recv_sem=recv.at[stage, step],
            device_id={"xline": peer_line},
            device_id_type=mesh_id,
        )

    def begin(step, _):
        across(step).start()
        return 0

    lax.fori_loop(1, columns, begin, 0)
    mine = pltpu.make_async_copy(running_ref.at[me], out_ref.at[line * columns + me], own.at[0])
    mine.start()
    mine.wait()
    onward(2, line, far_line, 0).start()
    onward(1, line, core_line, 0).start()

    def relay(step, _):
        slot = line * columns + lax.rem(me + columns - step, columns)
        pltpu.make_async_remote_copy(
            src_ref=out_ref.at[slot],
            dst_ref=out_ref.at[slot],
            send_sem=send.at[0, step],
            recv_sem=recv.at[0, step],
            device_id={"shot": lax.rem(me + columns - step, columns)},
            device_id_type=mesh_id,
        ).wait_recv()
        onward(2, line, far_line, step).start()
        onward(1, line, core_line, step).start()
        return 0

    lax.fori_loop(1, columns, relay, 0)

    def turn(step, _):
        onward(2, far_line, far_line, step).wait_recv()
        onward(3, far_line, core_line, step).start()
        return 0

    lax.fori_loop(0, columns, turn, 0)

    def finish(step, _):
        onward(1, core_line, core_line, step).wait_recv()
        onward(3, diagonal_line, core_line, step).wait_recv()
        onward(1, line, core_line, step).wait_send()
        onward(2, line, far_line, step).wait_send()
        onward(3, far_line, core_line, step).wait_send()
        return 0

    lax.fori_loop(0, columns, finish, 0)

    def sent(step, _):
        across(step).wait_send()
        return 0

    lax.fori_loop(1, columns, sent, 0)


def xor_of(index, step):
    return lax.bitwise_xor(jnp.int32(index), jnp.int32(step))


def fused_kernel(
    lines, columns, bins, low,
    records_ref, targets_ref, aperture_ref, out_ref,
    records, table, inverse, expand, mixing, apertures, traces_here, traces,
    sent, spectra, picked_here, picked, running, gathered, raw, stage, result,
    load, own, near_send, near_recv, wide_send, wide_recv, run_send, run_recv, store,
):
    f32, bf16 = jnp.float32, jnp.bfloat16
    devices = lines * columns
    halves = records.shape[0]
    time_rows, shots, receivers = targets_ref.shape
    held = records_ref.shape[0] // receivers
    part = receivers // halves
    gathers = aperture_ref.shape[1]
    chosen = shots * gathers
    width = 2 * chosen
    rows = columns * bins
    depth = 2 * bins
    line = lax.axis_index("xline")
    shot_here = lax.axis_index("shot")
    me = line * columns + shot_here
    mesh_id = pl.DeviceIdType.MESH
    barrier = pltpu.get_barrier_semaphore()

    def greet(step, _):
        peer = lax.rem(me + step, devices)
        pl.semaphore_signal(
            barrier, inc=1,
            device_id={"xline": peer // columns, "shot": lax.rem(peer, columns)},
            device_id_type=mesh_id,
        )
        return 0

    lax.fori_loop(1, devices, greet, 0)

    loads = []
    for h in range(halves):
        for g in range(held):
            loads.append(
                pltpu.make_async_copy(
                    records_ref.at[pl.ds(g * receivers + h * part, part), :],
                    records.at[h, pl.ds(g * part, part), :],
                    load.at[h, g],
                )
            )
    for copy in loads:
        copy.start()
    raw_load = pltpu.make_async_copy(targets_ref, raw, own.at[7])
    raw_load.start()

    group = 4 * depth // 2
    scale = 1.0 / math.sqrt(NT)
    step_angle = 2.0 * math.pi / NT
    row = lax.broadcasted_iota(jnp.int32, (group, 128), 0)
    lane = lax.broadcasted_iota(jnp.int32, (group, 128), 1)
    freq = row // depth * bins + row % bins + 1
    turn = (row // bins % 2) * (NT // 4)
    group_bins = group // depth * bins

    def wave(first_freq, first_time):
        angle = ((freq + first_freq) * (lane + first_time) + turn) % NT
        return jnp.cos(angle.astype(f32) * step_angle) * scale

    across_time = 2.0 * jnp.cos((freq * 128 % NT).astype(f32) * step_angle)
    across_rows = 2.0 * jnp.cos((lane * group_bins % NT).astype(f32) * step_angle)
    flip = (1 - 2 * (freq % 2)).astype(f32)

    def fill(block, carry):
        at0, next0, at1, next1 = carry
        here = pl.ds(pl.multiple_of(block * group, group), group)
        now, later = at0, at1
        for k in range(NT // 256):
            table[here, k * 128 : (k + 1) * 128] = now.astype(bf16)
            table[here, NT // 2 + k * 128 : NT // 2 + (k + 1) * 128] = (now * flip).astype(bf16)
            now, later = later, across_time * later - now
        return next0, across_rows * next0 - at0, next1, across_rows * next1 - at1

    lax.fori_loop(
        0, 2 * NF // group, fill,
        (wave(0, 0), wave(group_bins, 0), wave(0, 128), wave(group_bins, 128)),
    )

    def transform(h):
        for g in range(held):
            loads[h * held + g].wait()
        value = lax.dot_general(
            table[...], records[h], (((1,), (1,)), ((), ())), preferred_element_type=f32
        )
        sent[h] = value.astype(bf16).reshape(sent.shape[1:])

    def wide(which, source, target, step):
        far, near = step // 8, lax.rem(step, 8)
        line_step = near // 4 * 2 + lax.rem(near, 2)
        shot_step = far * 2 + lax.rem(near // 2, 2)
        peer_line, peer_shot = xor_of(line, line_step), xor_of(shot_here, shot_step)
        return pltpu.make_async_remote_copy(
            src_ref=source.at[peer_line * columns + peer_shot],
            dst_ref=target.at[me],
            send_sem=wide_send.at[which, step],
            recv_sem=wide_recv.at[which, step],
            device_id={"xline": peer_line, "shot": peer_shot},
            device_id_type=mesh_id,
        )

    def wide_copy(which, step):
        if which < halves:
            return wide(which, sent.at[which], spectra.at[which], step)
        return wide(which, picked_here, picked, step)

    def start_wide(which, first, last):
        def begin(j, _):
            wide_copy(which, devices - 1 - j).start()
            return 0

        lax.fori_loop(first, last, begin, 0)

    def wait_wide(which):
        def finish(j, _):
            wide_copy(which, devices - 1 - j).wait()
            return 0

        lax.fori_loop(0, devices - 1, finish, 0)

    def along_line(which, step):
        peer = xor_of(line, step)
        source = traces_here.at[peer] if which else aperture_ref
        target = traces if which else apertures
        return pltpu.make_async_remote_copy(
            src_ref=source,
            dst_ref=target.at[line],
            send_sem=near_send.at[which, step],
            recv_sem=near_recv.at[which, step],
            device_id={"xline": peer},
            device_id_type=mesh_id,
        )

    def unpack_targets():
        raw_load.wait()
        rows = time_rows // 4
        for c in range(4):
            value = raw[c * rows : (c + 1) * rows].astype(f32)
            value = value.reshape(rows * shots, receivers)
            for h in range(halves):
                stage[h, c * rows * shots : (c + 1) * rows * shots, :] = value[:, h * part : (h + 1) * part]

    transform(0)
    unpack_targets()
    pl.semaphore_wait(barrier, devices - 1)
    for step in range(1, lines):
        along_line(0, step).start()
    start_wide(0, 0, devices - 1)
    mine = [
        pltpu.make_async_copy(aperture_ref, apertures.at[line], own.at[0]),
        pltpu.make_async_copy(sent.at[0, me], spectra.at[0, me], own.at[1]),
    ]
    for copy in mine:
        copy.start()
    transform(1)
    keep_one = pltpu.make_async_copy(sent.at[1, me], spectra.at[1, me], own.at[2])
    keep_one.start()
    for copy in mine:
        copy.wait()
    for step in range(1, lines):
        along_line(0, step).wait()

    wanted = []
    for l in range(lines):
        wanted += [apertures[l, s : s + 1, :] for s in range(shots)] * 2
    wanted = jnp.concatenate(wanted, axis=1)
    lane = lax.broadcasted_iota(jnp.int32, (receivers, lines * width), 1)
    receiver = lax.broadcasted_iota(jnp.int32, (receivers, lines * width), 0)
    total = jnp.zeros((time_rows, lines * width), f32)
    for shot in range(shots):
        hit = (lane % chosen // gathers == shot) & (receiver == wanted)
        onehot = jnp.where(hit, 1.0, 0.0).astype(bf16)
        for h in range(halves):
            total += jnp.dot(
                stage[h, pl.ds(shot, time_rows, stride=shots), :].astype(bf16),
                onehot[h * part : (h + 1) * part], preferred_element_type=f32,
            )
    fold = time_rows // 2
    lane = lax.broadcasted_iota(jnp.int32, (fold, lines * width), 1)
    folded = jnp.where(lane % width < chosen, total[:fold], total[fold:]).astype(bf16)
    for l in range(lines):
        traces_here[l] = folded[:, l * width : (l + 1) * width]
    for step in range(1, lines):
        along_line(1, step).start()
    keep = pltpu.make_async_copy(traces_here.at[line], traces.at[line], own.at[3])
    keep.start()
    start_wide(1, 0, low)

    taken = width
    across = held * columns * depth
    for shot in range(shots):
        for q in range(2):
            k = lax.broadcasted_iota(jnp.int32, (taken, held * columns * depth), 0)
            j = lax.broadcasted_iota(jnp.int32, (taken, held * columns * depth), 1)
            k_imag, k_shot, k_gather = k // chosen, k // gathers % shots, k % gathers
            j_held, j_column, j_imag = j // (columns * depth), j // depth % columns, j // bins % 2
            hit = (k_gather == j_column * held + j_held) & (k_shot == shot)
            hit = hit & ((k_imag != j_imag) if q else (k_imag == j_imag))
            value = jnp.where(hit, 1.0, 0.0)
            if q == 0:
                value = jnp.where(j_imag == 1, -value, value)
            expand[shot * 2 + q] = value.astype(bf16)
    slab = line * time_rows
    for c in range(time_rows // 128):
        block = table[:, pl.ds(pl.multiple_of(slab + c * 128, 128), 128)].astype(f32)
        inverse[c * 128 : (c + 1) * 128, :] = (block * 2.0).T.astype(bf16)

    keep.wait()
    for step in range(1, lines):
        along_line(1, step).wait()
    ahead = jnp.zeros((2 * NF, width), f32)
    behind = jnp.zeros((2 * NF, width), f32)
    for l in range(lines):
        base = l * time_rows
        ahead += jnp.dot(table[:, base : base + fold], traces[l], preferred_element_type=f32)
        behind += jnp.dot(
            table[:, base + fold : base + time_rows], traces[l], preferred_element_type=f32
        )
    real = (ahead + pltpu.roll(behind, chosen, 1)).reshape(devices, depth, width)[:, :bins]
    imag = (pltpu.roll(ahead, chosen, 1) + behind).reshape(devices, depth, width)[:, bins:]
    lane = lax.broadcasted_iota(jnp.int32, (devices, bins, width), 2)
    picked_here[...] = jnp.where(lane < chosen, real, imag).astype(bf16)
    start_wide(2, 0, devices - 1)
    start_wide(1, low, devices - 1)
    keep = pltpu.make_async_copy(picked_here.at[me], picked.at[me], own.at[4])
    keep.start()

    wait_wide(0)
    keep.wait()
    wait_wide(2)

    same_bin = (
        lax.broadcasted_iota(jnp.int32, (rows, across), 0) % bins
        == lax.broadcasted_iota(jnp.int32, (rows, across), 1) % bins
    )
    span = columns * depth
    for l in range(lines):
        block = picked[l * columns : (l + 1) * columns].astype(f32).reshape(rows, width).astype(bf16)
        for sq in range(2 * shots):
            value = jnp.dot(block, expand[sq], preferred_element_type=f32)
            value = jnp.where(same_bin, value, 0.0).astype(bf16)
            for g in range(held):
                first = (g * lines + l) * span
                mixing[sq * rows : (sq + 1) * rows, first : first + span] = (
                    value[:, g * span : (g + 1) * span]
                )

    def hop(h, stage, source_line, peer_line, step):
        slot = source_line * columns + xor_of(shot_here, step)
        return pltpu.make_async_remote_copy(
            src_ref=gathered.at[h, slot],
            dst_ref=gathered.at[h, slot],
            send_sem=run_send.at[h, stage, step],
            recv_sem=run_recv.at[h, stage, step],
            device_id={"xline": peer_line},
            device_id_type=mesh_id,
        )

    def spread(h, step):
        peer = xor_of(shot_here, step)
        return pltpu.make_async_remote_copy(
            src_ref=running.at[h, peer],
            dst_ref=gathered.at[h, me],
            send_sem=run_send.at[h, 0, step],
            recv_sem=run_recv.at[h, 0, step],
            device_id={"shot": peer},
            device_id_type=mesh_id,
        )

    core_line = xor_of(line, 1)
    far_line = xor_of(line, 2)
    diagonal_line = xor_of(line, 3)

    def mix(h):
        total = jnp.zeros((2 * shots * rows, part), f32)
        for g in range(held):
            block = spectra[h, :, :, g * part : (g + 1) * part].reshape(2 * NF, part)
            total += jnp.dot(
                mixing[:, g * 2 * NF : (g + 1) * 2 * NF], block, preferred_element_type=f32
            )
        for column in range(columns):
            for shot in range(shots):
                pieces = [
                    total[(shot * 2 + q) * rows + column * bins :][:bins] for q in range(2)
                ]
                running[h, column, shot] = jnp.concatenate(pieces, axis=0).astype(bf16)

        def begin(j, _):
            spread(h, columns - 1 - j).start()
            return 0

        lax.fori_loop(0, columns - 1, begin, 0)
        keep = pltpu.make_async_copy(running.at[h, shot_here], gathered.at[h, me], own.at[5 + h])
        keep.start()
        keep.wait()
        hop(h, 2, line, far_line, 0).start()
        hop(h, 1, line, core_line, 0).start()

    def relay(h):
        def pass_on(j, _):
            step = j + 1
            spread(h, step).wait()
            hop(h, 2, line, far_line, step).start()
            hop(h, 1, line, core_line, step).start()
            return 0

        lax.fori_loop(0, columns - 1, pass_on, 0)

    def turn_over(h):
        def pass_on(step, _):
            hop(h, 2, far_line, far_line, step).wait_recv()
            hop(h, 3, far_line, core_line, step).start()
            return 0

        lax.fori_loop(0, columns, pass_on, 0)

    def complete(h):
        def finish(step, _):
            hop(h, 1, core_line, core_line, step).wait_recv()
            hop(h, 3, diagonal_line, core_line, step).wait_recv()
            hop(h, 1, line, core_line, step).wait_send()
            hop(h, 2, line, far_line, step).wait_send()
            hop(h, 3, far_line, core_line, step).wait_send()
            return 0

        lax.fori_loop(0, columns, finish, 0)

    def invert(h):
        for shot in range(shots):
            block = gathered[h, :, shot].reshape(2 * NF, part)
            stage[h, pl.ds(shot, time_rows, stride=shots), :] = jnp.dot(
                inverse[...], block, preferred_element_type=f32
            )

    pieces = 4

    def put(h, c):
        rows = time_rows // pieces
        here = (pl.ds(c * rows, rows), slice(None), pl.ds(h * part, part))
        return pltpu.make_async_copy(result.at[here], out_ref.at[here], store.at[h, c])

    def emit(h):
        rows = time_rows // pieces
        lanes = slice(h * part, (h + 1) * part)
        for c in range(pieces):
            value = stage[h, c * rows * shots : (c + 1) * rows * shots, :]
            result[c * rows : (c + 1) * rows, :, lanes] = value.reshape(rows, shots, part).astype(bf16)
            put(h, c).start()

    def settle(h):
        for c in range(pieces):
            put(h, c).wait()

    mix(0)
    keep_one.wait()
    wait_wide(1)
    mix(1)
    relay(0)
    turn_over(0)
    relay(1)
    complete(0)
    invert(0)
    emit(0)
    turn_over(1)
    complete(1)
    invert(1)
    emit(1)
    settle(0)
    settle(1)


def fused(records, targets, aperture):
    bf16 = jnp.bfloat16
    lines = lax.axis_size("xline")
    columns = lax.axis_size("shot")
    devices = lines * columns
    bins = NF // devices
    time_rows, shots, receivers = targets.shape
    held = records.shape[1]
    gathers = aperture.shape[2]
    halves, part = 2, receivers // 2
    width = 2 * shots * gathers
    wide = held * columns * 2 * bins
    in_vmem = pl.BlockSpec(memory_space=pltpu.VMEM)
    any_place = pl.BlockSpec(memory_space=pl.ANY)
    dma = pltpu.SemaphoreType.DMA
    vmem = lambda *shape: pltpu.VMEM(shape, bf16)
    out = pl.pallas_call(
        functools.partial(fused_kernel, lines, columns, bins, 10),
        out_shape=jax.ShapeDtypeStruct((time_rows, shots, receivers), bf16),
        in_specs=[any_place, any_place, in_vmem],
        out_specs=any_place,
        scratch_shapes=[
            vmem(halves, held * part, NT),
            vmem(2 * NF, NT),
            vmem(time_rows, 2 * NF),
            vmem(2 * shots, width, wide),
            vmem(2 * shots * columns * bins, lines * wide),
            pltpu.VMEM((lines, shots, gathers), jnp.int32),
            vmem(lines, time_rows // 2, width),
            vmem(lines, time_rows // 2, width),
            vmem(halves, devices, 2 * bins, held * part),
            vmem(halves, devices, 2 * bins, held * part),
            vmem(devices, bins, width),
            vmem(devices, bins, width),
            vmem(halves, columns, shots, 2 * bins, part),
            vmem(halves, devices, shots, 2 * bins, part),
            vmem(time_rows, shots, receivers),
            pltpu.VMEM((halves, time_rows * shots, part), jnp.float32),
            vmem(time_rows, shots, receivers),
            dma((halves, held)), dma((8,)), dma((2, lines)), dma((2, lines)),
            dma((3, devices)), dma((3, devices)),
            dma((halves, 4, columns)), dma((halves, 4, columns)), dma((halves, 4)),
        ],
        compiler_params=pltpu.CompilerParams(collective_id=2, has_side_effects=True),
    )(records.reshape(held * receivers, NT), targets, aperture.reshape(shots, gathers))
    return out


def on_device(records, targets, aperture):
    f32, bf16 = jnp.float32, jnp.bfloat16
    lines = lax.axis_size("xline")
    columns = lax.axis_size("shot")
    devices = lines * columns
    bins = NF // devices
    time_rows, shots, receivers = targets.shape
    held = records.shape[1]
    gathers = aperture.shape[2]
    if (lines, columns, bins, 2 * shots * gathers, receivers) == (4, 8, 8, 128, 256):
        return fused(records, targets, aperture)
    table = fourier_table(bins, 0, NT)
    chosen = shots * gathers
    padded = -(-chosen // 128) * 128

    spectra = jnp.einsum(
        "tp,kt->pk", table, records.reshape(held * receivers, NT), preferred_element_type=f32
    ).astype(bf16)

    spectra = spectra.reshape(devices, 2 * bins, held * receivers)
    in_vmem = pl.BlockSpec(memory_space=pltpu.VMEM)
    dma = pltpu.SemaphoreType.DMA
    spectra, picked = pl.pallas_call(
        functools.partial(spread_kernel, lines, columns, gathers),
        out_shape=[
            jax.ShapeDtypeStruct(spectra.shape, bf16),
            jax.ShapeDtypeStruct((devices, 2 * bins, padded), bf16),
        ],
        in_specs=[in_vmem] * 4,
        out_specs=[in_vmem] * 2,
        scratch_shapes=[
            pltpu.VMEM((lines, shots, gathers), jnp.int32),
            pltpu.VMEM((lines, time_rows, padded), bf16),
            pltpu.VMEM((lines, time_rows, padded), bf16),
            pltpu.VMEM((devices, 2 * bins, padded), bf16),
            dma((2, devices)), dma((2, devices)), dma((4,)), dma((2, lines)), dma((2, lines)),
        ],
        compiler_params=pltpu.CompilerParams(collective_id=0, has_side_effects=True),
    )(spectra, targets.transpose(1, 0, 2), aperture.reshape(shots, gathers), table)
    picked = picked.reshape(devices, 2, bins, padded)[..., :chosen]
    picked = jnp.concatenate([picked[:, 0], picked[:, 1]], axis=-1)

    running = pl.pallas_call(
        functools.partial(mix_kernel, lines, columns, held, bins, shots),
        out_shape=jax.ShapeDtypeStruct((shots * 2 * columns * bins, receivers), bf16),
        in_specs=[pl.BlockSpec(memory_space=pltpu.VMEM)] * 2,
        out_specs=pl.BlockSpec(memory_space=pltpu.VMEM),
    )(spectra.reshape(2 * NF, held * receivers), picked.reshape(NF, -1))
    running = running.reshape(shots, 2, columns, bins, receivers).transpose(2, 0, 1, 3, 4)
    running = running.reshape(columns, shots, 2 * bins, receivers)
    running = pl.pallas_call(
        functools.partial(collect_kernel, lines, columns),
        out_shape=jax.ShapeDtypeStruct((devices, *running.shape[1:]), bf16),
        in_specs=[in_vmem],
        out_specs=in_vmem,
        scratch_shapes=[dma((4, columns)), dma((4, columns)), dma((1,))],
        compiler_params=pltpu.CompilerParams(collective_id=1, has_side_effects=True),
    )(running)
    running = running.transpose(0, 2, 1, 3).reshape(2 * NF, shots, receivers)

    rows = fourier_table(bins, lax.axis_index("xline") * time_rows, time_rows)
    out = jnp.einsum("tp,psr->tsr", rows * 2, running, preferred_element_type=f32)
    return out.astype(bf16)


def solution(mesh):
    in_specs = (P("xline", "shot", None, None), P("xline", "shot", None), P("shot", "xline", None))
    out_specs = P("xline", "shot", None)
    return jax.shard_map(
        on_device, mesh=mesh, in_specs=in_specs, out_specs=out_specs, check_vma=False
    )
```

```python
import functools
import math

import jax
import jax.numpy as jnp
from jax import lax
from jax.experimental import pallas as pl
from jax.experimental.pallas import tpu as pltpu
from jax.sharding import PartitionSpec as P

NT = 2048
NF = 256
LOW = 32


def fourier_table(bins, start, count):
    blocks = NF // bins
    freq = jnp.arange(1, NF + 1, dtype=jnp.int32).reshape(blocks, 1, bins)
    freq = jnp.broadcast_to(freq, (blocks, 2, bins)).reshape(1, 2 * NF)
    is_imag = jnp.arange(2, dtype=jnp.int32).reshape(1, 2, 1)
    is_imag = jnp.broadcast_to(is_imag, (blocks, 2, bins)).reshape(1, 2 * NF) == 1

    def trig(times):
        angles = (times[:, None] * freq % NT).astype(jnp.float32) * (2.0 * math.pi / NT)
        return jnp.cos(angles), jnp.sin(angles)

    cos_hi, sin_hi = trig(start + jnp.arange(count // LOW, dtype=jnp.int32) * LOW)
    cos_lo, sin_lo = trig(jnp.arange(LOW, dtype=jnp.int32))
    scale = 1.0 / math.sqrt(NT)
    first = jnp.where(is_imag, -sin_hi, cos_hi) * scale
    second = jnp.where(is_imag, -cos_hi, -sin_hi) * scale
    first, second, cos_lo, sin_lo = lax.optimization_barrier((first, second, cos_lo, sin_lo))
    table = first[:, None] * cos_lo[None] + second[:, None] * sin_lo[None]
    return table.reshape(count, 2 * NF).astype(jnp.bfloat16)


def mix_kernel(lines, columns, held, bins, shots, spectra_ref, picked_ref, out_ref):
    gathers = columns * held
    receivers = out_ref.shape[1]
    rows = columns * bins
    depth = columns * 2 * bins
    taken = 2 * shots * gathers
    wide = held * depth

    k = lax.broadcasted_iota(jnp.int32, (taken, wide), 0)
    j = lax.broadcasted_iota(jnp.int32, (taken, wide), 1)
    k_imag, k_shot, k_gather = k // (shots * gathers), k // gathers % shots, k % gathers
    j_held, j_column, j_imag = j // depth, j % depth // (2 * bins), j // bins % 2
    same = k_gather == j_column * held + j_held
    crossed = k_imag != j_imag
    expand = []
    for shot in range(shots):
        for part in range(2):
            hit = same & (k_shot == shot) & (crossed if part else ~crossed)
            value = jnp.where(hit, 1.0, 0.0)
            if part == 0:
                value = jnp.where(j_imag == 1, -value, value)
            expand.append(value.astype(jnp.bfloat16))
    bin_of_row = lax.broadcasted_iota(jnp.int32, (rows, wide), 0) % bins
    bin_of_column = lax.broadcasted_iota(jnp.int32, (rows, wide), 1) % bins
    same_bin = bin_of_row == bin_of_column

    total = jnp.zeros(out_ref.shape, jnp.float32)
    for line in range(lines):
        block = picked_ref[line * rows : (line + 1) * rows, :]
        mixing = [
            jnp.where(
                same_bin, jnp.dot(block, matrix, preferred_element_type=jnp.float32), 0.0
            ).astype(jnp.bfloat16)
            for matrix in expand
        ]
        held_rows = slice(line * depth, (line + 1) * depth)
        spectra = jnp.concatenate(
            [spectra_ref[held_rows, h * receivers : (h + 1) * receivers] for h in range(held)], axis=0
        )
        total += jnp.dot(
            jnp.concatenate(mixing, axis=0), spectra, preferred_element_type=jnp.float32
        )
    out_ref[...] = total.astype(out_ref.dtype)


def spread_kernel(
    lines, columns, gathers, spectra_ref, targets_ref, aperture_ref, table_ref,
    spectra_out, picked_out,
    apertures, traces_here, traces, picked, send, recv, own, line_send, line_recv,
):
    devices = lines * columns
    line = lax.axis_index("xline")
    shot_here = lax.axis_index("shot")
    shots, time_rows, receivers = targets_ref.shape
    width = traces.shape[2]
    me = lax.axis_index("xline") * columns + lax.axis_index("shot")
    mesh_id = pl.DeviceIdType.MESH
    barrier = pltpu.get_barrier_semaphore()

    def greet(step, _):
        peer = lax.rem(me + step, devices)
        pl.semaphore_signal(
            barrier, inc=1,
            device_id={"xline": peer // columns, "shot": lax.rem(peer, columns)},
            device_id_type=mesh_id,
        )
        return 0

    lax.fori_loop(1, devices, greet, 0)
    pl.semaphore_wait(barrier, devices - 1)

    def line_of(step):
        far, other = step // columns // 2, lax.rem(step // columns, 2)
        moved = lax.rem(line + far * (lines // 2), lines)
        return moved + other * (1 - 2 * lax.rem(moved, 2))

    def copy_of(which, source, target, step):
        peer = line_of(step) * columns + lax.rem(shot_here + step, columns)
        return pltpu.make_async_remote_copy(
            src_ref=source.at[peer],
            dst_ref=target.at[me],
            send_sem=send.at[which, step],
            recv_sem=recv.at[which, step],
            device_id={"xline": peer // columns, "shot": lax.rem(peer, columns)},
            device_id_type=mesh_id,
        )

    def arrival_of(which, target, step):
        origin = line_of(step) * columns + lax.rem(shot_here + devices - step, columns)
        return pltpu.make_async_remote_copy(
            src_ref=target.at[origin],
            dst_ref=target.at[origin],
            send_sem=send.at[which, step],
            recv_sem=recv.at[which, step],
            device_id={"xline": origin // columns, "shot": lax.rem(origin, columns)},
            device_id_type=mesh_id,
        )

    def along_line(which, source, target, step):
        peer = lax.rem(line + step, lines)
        return pltpu.make_async_remote_copy(
            src_ref=source.at[peer] if which else source,
            dst_ref=target.at[line],
            send_sem=line_send.at[which, step],
            recv_sem=line_recv.at[which, step],
            device_id={"xline": peer},
            device_id_type=mesh_id,
        )

    def from_line(which, target, step):
        origin = lax.rem(line + lines - step, lines)
        return pltpu.make_async_remote_copy(
            src_ref=target.at[origin],
            dst_ref=target.at[origin],
            send_sem=line_send.at[which, step],
            recv_sem=line_recv.at[which, step],
            device_id={"xline": origin},
            device_id_type=mesh_id,
        )

    def begin(step, _):
        copy_of(0, spectra_ref, spectra_out, step).start()
        return 0

    for step in range(1, lines):
        along_line(0, aperture_ref, apertures, step).start()
    lax.fori_loop(1, 2 * columns, begin, 0)
    mine = [
        pltpu.make_async_copy(aperture_ref, apertures.at[line], own.at[0]),
        pltpu.make_async_copy(spectra_ref.at[me], spectra_out.at[me], own.at[1]),
    ]
    for copy in mine:
        copy.start()
    for copy in mine:
        copy.wait()
    for step in range(1, lines):
        from_line(0, apertures, step).wait_recv()

    wanted = []
    for l in range(lines):
        wanted += [apertures[l, s : s + 1, :] for s in range(shots)]
        if width > shots * gathers:
            wanted.append(jnp.zeros((1, width - shots * gathers), jnp.int32))
    wanted = jnp.concatenate(wanted, axis=1)
    lane = lax.broadcasted_iota(jnp.int32, (receivers, lines * width), 1)
    receiver = lax.broadcasted_iota(jnp.int32, (receivers, lines * width), 0)
    total = jnp.zeros((time_rows, lines * width), jnp.float32)
    for shot in range(shots):
        hit = (lane % width // gathers == shot) & (receiver == wanted)
        onehot = jnp.where(hit, 1.0, 0.0).astype(jnp.bfloat16)
        total += jnp.dot(targets_ref[shot], onehot, preferred_element_type=jnp.float32)
    total = total.astype(jnp.bfloat16)
    for l in range(lines):
        traces_here[l] = total[:, l * width : (l + 1) * width]

    arrival_of(0, spectra_out, 1).wait_recv()
    for step in range(1, lines):
        along_line(1, traces_here, traces, step).start()
    lax.fori_loop(2 * columns, devices, begin, 0)
    keep = pltpu.make_async_copy(traces_here.at[line], traces.at[line], own.at[2])
    keep.start()
    keep.wait()
    for step in range(1, lines):
        from_line(1, traces, step).wait_recv()

    value = jnp.zeros((table_ref.shape[1], width), jnp.float32)
    for l in range(lines):
        value += lax.dot_general(
            table_ref[l * time_rows : (l + 1) * time_rows, :], traces[l],
            (((0,), (0,)), ((), ())),
            preferred_element_type=jnp.float32,
        )
    picked[...] = value.astype(jnp.bfloat16).reshape(picked.shape)
    arrival_of(0, spectra_out, 2).wait_recv()

    def begin_picked(step, _):
        copy_of(1, picked, picked_out, step).start()
        return 0

    lax.fori_loop(1, devices, begin_picked, 0)
    keep = pltpu.make_async_copy(picked.at[me], picked_out.at[me], own.at[3])
    keep.start()
    keep.wait()
    for step in range(1, lines):
        along_line(0, aperture_ref, apertures, step).wait_send()
        along_line(1, traces_here, traces, step).wait_send()

    def finish(step, _):
        copy_of(0, spectra_ref, spectra_out, step).wait_send()
        copy_of(1, picked, picked_out, step).wait_send()
        arrival_of(1, picked_out, step).wait_recv()
        return 0

    def arrived(step, _):
        arrival_of(0, spectra_out, step).wait_recv()
        return 0

    lax.fori_loop(3, devices, arrived, 0)
    lax.fori_loop(1, devices, finish, 0)


def collect_kernel(lines, columns, running_ref, out_ref, send, recv, own):
    line = lax.axis_index("xline")
    me = lax.axis_index("shot")
    core_line = line + 1 - 2 * lax.rem(line, 2)
    far_line = lax.rem(line + lines // 2, lines)
    diagonal_line = lax.rem(core_line + lines // 2, lines)
    mesh_id = pl.DeviceIdType.MESH
    barrier = pltpu.get_barrier_semaphore()

    def greet(step, _):
        pl.semaphore_signal(
            barrier, inc=1, device_id={"shot": lax.rem(me + step, columns)}, device_id_type=mesh_id
        )
        return 0

    lax.fori_loop(1, columns, greet, 0)
    for peer in (core_line, far_line):
        pl.semaphore_signal(barrier, inc=1, device_id={"xline": peer}, device_id_type=mesh_id)
    pl.semaphore_wait(barrier, columns + 1)

    def across(step):
        peer = lax.rem(me + step, columns)
        return pltpu.make_async_remote_copy(
            src_ref=running_ref.at[peer],
            dst_ref=out_ref.at[line * columns + me],
            send_sem=send.at[0, step],
            recv_sem=recv.at[0, step],
            device_id={"shot": peer},
            device_id_type=mesh_id,
        )

    def onward(stage, source_line, peer_line, step):
        slot = source_line * columns + lax.rem(me + columns - step, columns)
        return pltpu.make_async_remote_copy(
            src_ref=out_ref.at[slot],
            dst_ref=out_ref.at[slot],
            send_sem=send.at[stage, step],
            recv_sem=recv.at[stage, step],
            device_id={"xline": peer_line},
            device_id_type=mesh_id,
        )

    def begin(step, _):
        across(step).start()
        return 0

    lax.fori_loop(1, columns, begin, 0)
    mine = pltpu.make_async_copy(running_ref.at[me], out_ref.at[line * columns + me], own.at[0])
    mine.start()
    mine.wait()
    onward(2, line, far_line, 0).start()
    onward(1, line, core_line, 0).start()

    def relay(step, _):
        slot = line * columns + lax.rem(me + columns - step, columns)
        pltpu.make_async_remote_copy(
            src_ref=out_ref.at[slot],
            dst_ref=out_ref.at[slot],
            send_sem=send.at[0, step],
            recv_sem=recv.at[0, step],
            device_id={"shot": lax.rem(me + columns - step, columns)},
            device_id_type=mesh_id,
        ).wait_recv()
        onward(2, line, far_line, step).start()
        onward(1, line, core_line, step).start()
        return 0

    lax.fori_loop(1, columns, relay, 0)

    def turn(step, _):
        onward(2, far_line, far_line, step).wait_recv()
        onward(3, far_line, core_line, step).start()
        return 0

    lax.fori_loop(0, columns, turn, 0)

    def finish(step, _):
        onward(1, core_line, core_line, step).wait_recv()
        onward(3, diagonal_line, core_line, step).wait_recv()
        onward(1, line, core_line, step).wait_send()
        onward(2, line, far_line, step).wait_send()
        onward(3, far_line, core_line, step).wait_send()
        return 0

    lax.fori_loop(0, columns, finish, 0)

    def sent(step, _):
        across(step).wait_send()
        return 0

    lax.fori_loop(1, columns, sent, 0)


def xor_of(index, step):
    return lax.bitwise_xor(jnp.int32(index), jnp.int32(step))


def fused_kernel(
    lines, columns, bins,
    records_ref, targets_ref, aperture_ref, out_ref,
    records, table, inverse, expand, mixing, apertures, traces_here, traces,
    sent, spectra, picked_here, picked, running, gathered, raw, stage, unpacked,
    load, own, near_send, near_recv, wide_send, wide_recv, run_send, across_recv, far_recv, core_recv,
):
    f32, bf16 = jnp.float32, jnp.bfloat16
    devices = lines * columns
    halves = records.shape[0]
    time_rows, shots, receivers = targets_ref.shape
    held = records_ref.shape[0] // receivers
    part = receivers // halves
    gathers = aperture_ref.shape[1]
    chosen = shots * gathers
    width = 2 * chosen
    rows = columns * bins
    depth = 2 * bins
    line = lax.axis_index("xline")
    shot_here = lax.axis_index("shot")
    me = line * columns + shot_here
    mesh_id = pl.DeviceIdType.MESH
    barrier = pltpu.get_barrier_semaphore()

    def greet(step, _):
        peer = lax.rem(me + step, devices)
        pl.semaphore_signal(
            barrier, inc=1,
            device_id={"xline": peer // columns, "shot": lax.rem(peer, columns)},
            device_id_type=mesh_id,
        )
        return 0

    lax.fori_loop(1, devices, greet, 0)

    loads = []
    for h in range(halves):
        for g in range(held):
            loads.append(
                pltpu.make_async_copy(
                    records_ref.at[pl.ds(g * receivers + h * part, part), :],
                    records.at[h, pl.ds(g * part, part), :],
                    load.at[h, g],
                )
            )
    for copy in loads:
        copy.start()
    raw_load = pltpu.make_async_copy(targets_ref, raw, own.at[7])
    raw_load.start()
    aperture_load = pltpu.make_async_copy(aperture_ref, apertures.at[line], own.at[0])
    aperture_load.start()

    group = 4 * depth // 2
    scale = 1.0 / math.sqrt(NT)
    step_angle = 2.0 * math.pi / NT
    row = lax.broadcasted_iota(jnp.int32, (group, 128), 0)
    lane = lax.broadcasted_iota(jnp.int32, (group, 128), 1)
    freq = row // depth * bins + row % bins + 1
    turn = (row // bins % 2) * (NT // 4)
    group_bins = group // depth * bins

    def wave(first_freq, first_time):
        angle = ((freq + first_freq) * (lane + first_time) + turn) % NT
        return jnp.cos(angle.astype(f32) * step_angle) * scale

    across_time = 2.0 * jnp.cos((freq * 128 % NT).astype(f32) * step_angle)
    across_rows = 2.0 * jnp.cos((lane * group_bins % NT).astype(f32) * step_angle)
    flip = (1 - 2 * (freq % 2)).astype(f32)

    def fill(block, carry):
        at0, next0, at1, next1 = carry
        here = pl.ds(pl.multiple_of(block * group, group), group)
        now, later = at0, at1
        for k in range(NT // 256):
            table[here, k * 128 : (k + 1) * 128] = now.astype(bf16)
            table[here, NT // 2 + k * 128 : NT // 2 + (k + 1) * 128] = (now * flip).astype(bf16)
            now, later = later, across_time * later - now
        return next0, across_rows * next0 - at0, next1, across_rows * next1 - at1

    lax.fori_loop(
        0, 2 * NF // group, fill,
        (wave(0, 0), wave(group_bins, 0), wave(0, 128), wave(group_bins, 128)),
    )

    def transform(h):
        for g in range(held):
            loads[h * held + g].wait()
        value = lax.dot_general(
            table[...], records[h], (((1,), (1,)), ((), ())), preferred_element_type=f32
        )
        sent[h] = value.astype(bf16).reshape(sent.shape[1:])

    def await_all(source, target, count, send_sem, recv_sem):
        copy = pltpu.make_async_remote_copy(
            src_ref=source.at[pl.ds(0, count)],
            dst_ref=target.at[pl.ds(0, count)],
            send_sem=send_sem,
            recv_sem=recv_sem,
            device_id={"xline": xor_of(line, 1)},
            device_id_type=mesh_id,
        )
        copy.wait()

    def wide(which, source, target, step):
        far, near = step // 8, lax.rem(step, 8)
        line_step = near // 4 * 2 + lax.rem(near, 2)
        shot_step = far * 2 + lax.rem(near // 2, 2)
        peer_line, peer_shot = xor_of(line, line_step), xor_of(shot_here, shot_step)
        return pltpu.make_async_remote_copy(
            src_ref=source.at[peer_line * columns + peer_shot],
            dst_ref=target.at[me],
            send_sem=wide_send.at[which],
            recv_sem=wide_recv.at[which],
            device_id={"xline": peer_line, "shot": peer_shot},
            device_id_type=mesh_id,
        )

    def wide_copy(which, step):
        if which < halves:
            return wide(which, sent.at[which], spectra.at[which], step)
        return wide(which, picked_here, picked, step)

    def start_wide(which, cross):
        def begin(j, _):
            wide_copy(which, (3 - j // 4) * 8 + cross * 4 + 3 - lax.rem(j, 4)).start()
            return 0

        lax.fori_loop(0, devices // 2 - 1 + cross, begin, 0)

    def wait_wide(which):
        if which < halves:
            source, target = sent.at[which], spectra.at[which]
        else:
            source, target = picked_here, picked
        await_all(source, target, devices - 1, wide_send.at[which], wide_recv.at[which])

    def along_line(which, step):
        peer = xor_of(line, step)
        source = traces_here.at[peer] if which else apertures.at[line]
        target = traces if which else apertures
        return pltpu.make_async_remote_copy(
            src_ref=source,
            dst_ref=target.at[line],
            send_sem=near_send.at[which * step],
            recv_sem=near_recv.at[which * step],
            device_id={"xline": peer},
            device_id_type=mesh_id,
        )

    def unpack_targets():
        raw_load.wait()
        rows = time_rows // 4
        for c in range(4):
            value = raw[c * rows : (c + 1) * rows].astype(f32)
            value = value.reshape(rows * shots, receivers)
            for h in range(halves):
                stage[h, c * rows * shots : (c + 1) * rows * shots, :] = value[:, h * part : (h + 1) * part]
        for shot in range(shots):
            for h in range(halves):
                unpacked[shot, :, h * part : (h + 1) * part] = (
                    stage[h, pl.ds(shot, time_rows, stride=shots), :].astype(bf16)
                )

    transform(0)
    unpack_targets()
    transform(1)
    taken = width
    across = held * columns * depth
    for shot in range(shots):
        for q in range(2):
            k = lax.broadcasted_iota(jnp.int32, (taken, held * columns * depth), 0)
            j = lax.broadcasted_iota(jnp.int32, (taken, held * columns * depth), 1)
            k_imag, k_shot, k_gather = k // chosen, k // gathers % shots, k % gathers
            j_held, j_column, j_imag = j // (columns * depth), j // depth % columns, j // bins % 2
            hit = (k_gather == j_column * held + j_held) & (k_shot == shot)
            hit = hit & ((k_imag != j_imag) if q else (k_imag == j_imag))
            value = jnp.where(hit, 1.0, 0.0)
            if q == 0:
                value = jnp.where(j_imag == 1, -value, value)
            expand[shot * 2 + q] = value.astype(bf16)
    slab = line * time_rows
    for c in range(time_rows // 128):
        block = table[:, pl.ds(pl.multiple_of(slab + c * 128, 128), 128)].astype(f32)
        inverse[c * 128 : (c + 1) * 128, :] = (block * 2.0).T.astype(bf16)

    aperture_load.wait()
    pl.semaphore_wait(barrier, devices - 1)
    for step in range(1, lines):
        along_line(0, step).start()
    start_wide(0, 0)
    start_wide(1, 0)
    mine = [
        pltpu.make_async_copy(sent.at[0, me], spectra.at[0, me], own.at[1]),
    ]
    for copy in mine:
        copy.start()
    keep_one = pltpu.make_async_copy(sent.at[1, me], spectra.at[1, me], own.at[2])
    keep_one.start()
    for copy in mine:
        copy.wait()
    await_all(apertures, apertures, lines - 1, near_send.at[0], near_recv.at[0])

    fold = time_rows // 2
    lane = lax.broadcasted_iota(jnp.int32, (fold, width), 1)
    receiver = lax.broadcasted_iota(jnp.int32, (receivers, width), 0)
    chosen_by = []
    for shot in range(shots):
        wanted = jnp.concatenate([apertures[l, shot : shot + 1, :] for l in range(lines)] * 2, axis=1)
        onehot = jnp.where(receiver == wanted, 1.0, 0.0).astype(bf16)
        value = jnp.dot(unpacked[shot], onehot, preferred_element_type=f32)
        chosen_by.append(jnp.where(lane < chosen, value[:fold], value[fold:]))
    for l in range(lines):
        value = chosen_by[l]
        for shot in range(shots):
            if shot != l:
                moved = pltpu.roll(chosen_by[shot], (shot - l) * gathers % width, 1)
                value = jnp.where(lane // gathers % shots == shot, moved, value)
        traces_here[l] = value.astype(bf16)
    for step in (2, 3, 1):
        along_line(1, step).start()
    keep = pltpu.make_async_copy(traces_here.at[line], traces.at[line], own.at[3])
    keep.start()
    start_wide(0, 1)

    keep.wait()
    ahead = jnp.zeros((2 * NF, width), f32)
    behind = jnp.zeros((2 * NF, width), f32)
    for step in range(lines):
        l = xor_of(line, step)
        if step:
            along_line(1, step).wait()
        base = pl.multiple_of(l * time_rows, time_rows)
        ahead += jnp.dot(table[:, pl.ds(base, fold)], traces[l], preferred_element_type=f32)
        behind += jnp.dot(table[:, pl.ds(base + fold, fold)], traces[l], preferred_element_type=f32)
    real = (ahead + pltpu.roll(behind, chosen, 1)).reshape(devices, depth, width)[:, :bins]
    imag = (pltpu.roll(ahead, chosen, 1) + behind).reshape(devices, depth, width)[:, bins:]
    lane = lax.broadcasted_iota(jnp.int32, (devices, bins, width), 2)
    picked_here[...] = jnp.where(lane < chosen, real, imag).astype(bf16)
    start_wide(2, 1)
    start_wide(2, 0)
    start_wide(1, 1)
    keep = pltpu.make_async_copy(picked_here.at[me], picked.at[me], own.at[4])
    keep.start()

    wait_wide(0)
    keep.wait()
    wait_wide(2)

    same_bin = (
        lax.broadcasted_iota(jnp.int32, (rows, across), 0) % bins
        == lax.broadcasted_iota(jnp.int32, (rows, across), 1) % bins
    )
    span = columns * depth
    for l in range(lines):
        block = picked[l * columns : (l + 1) * columns].astype(f32).reshape(rows, width).astype(bf16)
        for sq in range(2 * shots):
            value = jnp.dot(block, expand[sq], preferred_element_type=f32)
            value = jnp.where(same_bin, value, 0.0).astype(bf16)
            for g in range(held):
                first = (g * lines + l) * span
                mixing[sq * rows : (sq + 1) * rows, first : first + span] = (
                    value[:, g * span : (g + 1) * span]
                )

    def hop(h, stage, source_line, peer_line, step):
        slot = source_line * columns + xor_of(shot_here, step)
        return pltpu.make_async_remote_copy(
            src_ref=gathered.at[h, slot],
            dst_ref=gathered.at[h, slot],
            send_sem=run_send.at[h, stage],
            recv_sem=far_recv.at[h, step] if stage == 2 else core_recv.at[h, stage // 2],
            device_id={"xline": peer_line},
            device_id_type=mesh_id,
        )

    def spread(h, step):
        peer = xor_of(shot_here, step)
        return pltpu.make_async_remote_copy(
            src_ref=running.at[h, peer],
            dst_ref=gathered.at[h, me],
            send_sem=run_send.at[h, 0],
            recv_sem=across_recv.at[h, step],
            device_id={"shot": peer},
            device_id_type=mesh_id,
        )

    core_line = xor_of(line, 1)
    far_line = xor_of(line, 2)
    diagonal_line = xor_of(line, 3)

    def mix(h):
        total = jnp.zeros((2 * shots * rows, part), f32)
        for g in range(held):
            block = spectra[h, :, :, g * part : (g + 1) * part].reshape(2 * NF, part)
            total += jnp.dot(
                mixing[:, g * 2 * NF : (g + 1) * 2 * NF], block, preferred_element_type=f32
            )
        for column in range(columns):
            for shot in range(shots):
                pieces = [
                    total[(shot * 2 + q) * rows + column * bins :][:bins] for q in range(2)
                ]
                running[h, column, shot] = jnp.concatenate(pieces, axis=0).astype(bf16)

        def begin(j, _):
            spread(h, lax.select(j == 0, 1, columns - j)).start()
            return 0

        lax.fori_loop(0, columns - 1, begin, 0)
        keep = pltpu.make_async_copy(running.at[h, shot_here], gathered.at[h, me], own.at[5 + h])
        keep.start()
        keep.wait()
        hop(h, 2, line, far_line, 0).start()
        hop(h, 1, line, core_line, 0).start()

    def relay(h):
        def pass_on(j, _):
            step = lax.select(j == 0, 1, columns - j)
            spread(h, step).wait_recv()
            hop(h, 2, line, far_line, step).start()
            hop(h, 1, line, core_line, step).start()
            return 0

        lax.fori_loop(0, columns - 1, pass_on, 0)

    def turn_over(h):
        def pass_on(step, _):
            hop(h, 2, far_line, far_line, step).wait_recv()
            hop(h, 3, far_line, core_line, step).start()
            return 0

        lax.fori_loop(0, columns, pass_on, 0)

    def complete(h):
        def settled(stage, count):
            source = running.at[h, pl.ds(0, count)]
            return pltpu.make_async_remote_copy(
                src_ref=source,
                dst_ref=gathered.at[h, pl.ds(0, count)],
                send_sem=run_send.at[h, stage],
                recv_sem=core_recv.at[h, stage // 2],
                device_id={"xline": core_line},
                device_id_type=mesh_id,
            )

        settled(1, columns).wait()
        settled(3, columns).wait()
        settled(2, columns).wait_send()
        settled(0, columns - 1).wait_send()

    def invert(h):
        for shot in range(shots):
            block = gathered[h, :, shot].reshape(2 * NF, part)
            stage[h, pl.ds(shot, time_rows, stride=shots), :] = jnp.dot(
                inverse[...], block, preferred_element_type=f32
            )

    pieces = 4

    def emit(h):
        rows = time_rows // pieces
        lanes = slice(h * part, (h + 1) * part)
        for c in range(pieces):
            value = stage[h, c * rows * shots : (c + 1) * rows * shots, :]
            out_ref[c * rows : (c + 1) * rows, :, lanes] = value.reshape(rows, shots, part).astype(bf16)

    mix(0)
    keep_one.wait()
    wait_wide(1)
    mix(1)
    relay(0)
    turn_over(0)
    relay(1)
    complete(0)
    invert(0)
    emit(0)
    turn_over(1)
    complete(1)
    invert(1)
    emit(1)


def fused(records, targets, aperture):
    bf16 = jnp.bfloat16
    lines = lax.axis_size("xline")
    columns = lax.axis_size("shot")
    devices = lines * columns
    bins = NF // devices
    time_rows, shots, receivers = targets.shape
    held = records.shape[1]
    gathers = aperture.shape[2]
    halves, part = 2, receivers // 2
    width = 2 * shots * gathers
    wide = held * columns * 2 * bins
    stay = lambda array: pltpu.with_memory_space_constraint(array, pltpu.HBM)
    in_vmem = pl.BlockSpec(memory_space=pltpu.VMEM)
    in_hbm = pl.BlockSpec(memory_space=pltpu.HBM)
    dma = pltpu.SemaphoreType.DMA
    vmem = lambda *shape: pltpu.VMEM(shape, bf16)
    out = pl.pallas_call(
        functools.partial(fused_kernel, lines, columns, bins),
        out_shape=jax.ShapeDtypeStruct((time_rows, shots, receivers), bf16),
        in_specs=[in_hbm, in_hbm, in_hbm],
        out_specs=in_vmem,
        scratch_shapes=[
            vmem(halves, held * part, NT),
            vmem(2 * NF, NT),
            vmem(time_rows, 2 * NF),
            vmem(2 * shots, width, wide),
            vmem(2 * shots * columns * bins, lines * wide),
            pltpu.VMEM((lines, shots, gathers), jnp.int32),
            vmem(lines, time_rows // 2, width),
            vmem(lines, time_rows // 2, width),
            vmem(halves, devices, 2 * bins, held * part),
            vmem(halves, devices, 2 * bins, held * part),
            vmem(devices, bins, width),
            vmem(devices, bins, width),
            vmem(halves, columns, shots, 2 * bins, part),
            vmem(halves, devices, shots, 2 * bins, part),
            vmem(time_rows, shots, receivers),
            pltpu.VMEM((halves, time_rows * shots, part), jnp.float32),
            vmem(shots, time_rows, receivers),
            dma((halves, held)), dma((8,)), dma((lines,)), dma((lines,)), dma((3,)), dma((3,)),
            dma((halves, 4)), dma((halves, columns)), dma((halves, columns)), dma((halves, 2)),
        ],
        compiler_params=pltpu.CompilerParams(collective_id=2, has_side_effects=True, vmem_limit_bytes=24 << 20),
    )(stay(records.reshape(held * receivers, NT)), stay(targets), stay(aperture.reshape(shots, gathers)))
    return out


def on_device(records, targets, aperture):
    f32, bf16 = jnp.float32, jnp.bfloat16
    lines = lax.axis_size("xline")
    columns = lax.axis_size("shot")
    devices = lines * columns
    bins = NF // devices
    time_rows, shots, receivers = targets.shape
    held = records.shape[1]
    gathers = aperture.shape[2]
    if (lines, columns, bins, 2 * shots * gathers, receivers) == (4, 8, 8, 128, 256):
        return fused(records, targets, aperture)
    table = fourier_table(bins, 0, NT)
    chosen = shots * gathers
    padded = -(-chosen // 128) * 128

    spectra = jnp.einsum(
        "tp,kt->pk", table, records.reshape(held * receivers, NT), preferred_element_type=f32
    ).astype(bf16)

    spectra = spectra.reshape(devices, 2 * bins, held * receivers)
    in_vmem = pl.BlockSpec(memory_space=pltpu.VMEM)
    dma = pltpu.SemaphoreType.DMA
    spectra, picked = pl.pallas_call(
        functools.partial(spread_kernel, lines, columns, gathers),
        out_shape=[
            jax.ShapeDtypeStruct(spectra.shape, bf16),
            jax.ShapeDtypeStruct((devices, 2 * bins, padded), bf16),
        ],
        in_specs=[in_vmem] * 4,
        out_specs=[in_vmem] * 2,
        scratch_shapes=[
            pltpu.VMEM((lines, shots, gathers), jnp.int32),
            pltpu.VMEM((lines, time_rows, padded), bf16),
            pltpu.VMEM((lines, time_rows, padded), bf16),
            pltpu.VMEM((devices, 2 * bins, padded), bf16),
            dma((2, devices)), dma((2, devices)), dma((4,)), dma((2, lines)), dma((2, lines)),
        ],
        compiler_params=pltpu.CompilerParams(collective_id=0, has_side_effects=True),
    )(spectra, targets.transpose(1, 0, 2), aperture.reshape(shots, gathers), table)
    picked = picked.reshape(devices, 2, bins, padded)[..., :chosen]
    picked = jnp.concatenate([picked[:, 0], picked[:, 1]], axis=-1)

    running = pl.pallas_call(
        functools.partial(mix_kernel, lines, columns, held, bins, shots),
        out_shape=jax.ShapeDtypeStruct((shots * 2 * columns * bins, receivers), bf16),
        in_specs=[pl.BlockSpec(memory_space=pltpu.VMEM)] * 2,
        out_specs=pl.BlockSpec(memory_space=pltpu.VMEM),
    )(spectra.reshape(2 * NF, held * receivers), picked.reshape(NF, -1))
    running = running.reshape(shots, 2, columns, bins, receivers).transpose(2, 0, 1, 3, 4)
    running = running.reshape(columns, shots, 2 * bins, receivers)
    running = pl.pallas_call(
        functools.partial(collect_kernel, lines, columns),
        out_shape=jax.ShapeDtypeStruct((devices, *running.shape[1:]), bf16),
        in_specs=[in_vmem],
        out_specs=in_vmem,
        scratch_shapes=[dma((4, columns)), dma((4, columns)), dma((1,))],
        compiler_params=pltpu.CompilerParams(collective_id=1, has_side_effects=True),
    )(running)
    running = running.transpose(0, 2, 1, 3).reshape(2 * NF, shots, receivers)

    rows = fourier_table(bins, lax.axis_index("xline") * time_rows, time_rows)
    out = jnp.einsum("tp,psr->tsr", rows * 2, running, preferred_element_type=f32)
    return out.astype(bf16)


def solution(mesh):
    in_specs = (P("xline", "shot", None, None), P("xline", "shot", None), P("shot", "xline", None))
    out_specs = P("xline", "shot", None)
    return jax.shard_map(
        on_device, mesh=mesh, in_specs=in_specs, out_specs=out_specs, check_vma=False
    )
```

```python
import functools
import math

import jax
import jax.numpy as jnp
from jax import lax
from jax.experimental import pallas as pl
from jax.experimental.pallas import tpu as pltpu
from jax.sharding import PartitionSpec as P

NT = 2048
NF = 256
LOW = 32


def fourier_table(bins, start, count):
    blocks = NF // bins
    freq = jnp.arange(1, NF + 1, dtype=jnp.int32).reshape(blocks, 1, bins)
    freq = jnp.broadcast_to(freq, (blocks, 2, bins)).reshape(1, 2 * NF)
    is_imag = jnp.arange(2, dtype=jnp.int32).reshape(1, 2, 1)
    is_imag = jnp.broadcast_to(is_imag, (blocks, 2, bins)).reshape(1, 2 * NF) == 1

    def trig(times):
        angles = (times[:, None] * freq % NT).astype(jnp.float32) * (2.0 * math.pi / NT)
        return jnp.cos(angles), jnp.sin(angles)

    cos_hi, sin_hi = trig(start + jnp.arange(count // LOW, dtype=jnp.int32) * LOW)
    cos_lo, sin_lo = trig(jnp.arange(LOW, dtype=jnp.int32))
    scale = 1.0 / math.sqrt(NT)
    first = jnp.where(is_imag, -sin_hi, cos_hi) * scale
    second = jnp.where(is_imag, -cos_hi, -sin_hi) * scale
    first, second, cos_lo, sin_lo = lax.optimization_barrier((first, second, cos_lo, sin_lo))
    table = first[:, None] * cos_lo[None] + second[:, None] * sin_lo[None]
    return table.reshape(count, 2 * NF).astype(jnp.bfloat16)


def mix_kernel(lines, columns, held, bins, shots, spectra_ref, picked_ref, out_ref):
    gathers = columns * held
    receivers = out_ref.shape[1]
    rows = columns * bins
    depth = columns * 2 * bins
    taken = 2 * shots * gathers
    wide = held * depth

    k = lax.broadcasted_iota(jnp.int32, (taken, wide), 0)
    j = lax.broadcasted_iota(jnp.int32, (taken, wide), 1)
    k_imag, k_shot, k_gather = k // (shots * gathers), k // gathers % shots, k % gathers
    j_held, j_column, j_imag = j // depth, j % depth // (2 * bins), j // bins % 2
    same = k_gather == j_column * held + j_held
    crossed = k_imag != j_imag
    expand = []
    for shot in range(shots):
        for part in range(2):
            hit = same & (k_shot == shot) & (crossed if part else ~crossed)
            value = jnp.where(hit, 1.0, 0.0)
            if part == 0:
                value = jnp.where(j_imag == 1, -value, value)
            expand.append(value.astype(jnp.bfloat16))
    bin_of_row = lax.broadcasted_iota(jnp.int32, (rows, wide), 0) % bins
    bin_of_column = lax.broadcasted_iota(jnp.int32, (rows, wide), 1) % bins
    same_bin = bin_of_row == bin_of_column

    total = jnp.zeros(out_ref.shape, jnp.float32)
    for line in range(lines):
        block = picked_ref[line * rows : (line + 1) * rows, :]
        mixing = [
            jnp.where(
                same_bin, jnp.dot(block, matrix, preferred_element_type=jnp.float32), 0.0
            ).astype(jnp.bfloat16)
            for matrix in expand
        ]
        held_rows = slice(line * depth, (line + 1) * depth)
        spectra = jnp.concatenate(
            [spectra_ref[held_rows, h * receivers : (h + 1) * receivers] for h in range(held)], axis=0
        )
        total += jnp.dot(
            jnp.concatenate(mixing, axis=0), spectra, preferred_element_type=jnp.float32
        )
    out_ref[...] = total.astype(out_ref.dtype)


def spread_kernel(
    lines, columns, gathers, spectra_ref, targets_ref, aperture_ref, table_ref,
    spectra_out, picked_out,
    apertures, traces_here, traces, picked, send, recv, own, line_send, line_recv,
):
    devices = lines * columns
    line = lax.axis_index("xline")
    shot_here = lax.axis_index("shot")
    shots, time_rows, receivers = targets_ref.shape
    width = traces.shape[2]
    me = lax.axis_index("xline") * columns + lax.axis_index("shot")
    mesh_id = pl.DeviceIdType.MESH
    barrier = pltpu.get_barrier_semaphore()

    def greet(step, _):
        peer = lax.rem(me + step, devices)
        pl.semaphore_signal(
            barrier, inc=1,
            device_id={"xline": peer // columns, "shot": lax.rem(peer, columns)},
            device_id_type=mesh_id,
        )
        return 0

    lax.fori_loop(1, devices, greet, 0)
    pl.semaphore_wait(barrier, devices - 1)

    def line_of(step):
        far, other = step // columns // 2, lax.rem(step // columns, 2)
        moved = lax.rem(line + far * (lines // 2), lines)
        return moved + other * (1 - 2 * lax.rem(moved, 2))

    def copy_of(which, source, target, step):
        peer = line_of(step) * columns + lax.rem(shot_here + step, columns)
        return pltpu.make_async_remote_copy(
            src_ref=source.at[peer],
            dst_ref=target.at[me],
            send_sem=send.at[which, step],
            recv_sem=recv.at[which, step],
            device_id={"xline": peer // columns, "shot": lax.rem(peer, columns)},
            device_id_type=mesh_id,
        )

    def arrival_of(which, target, step):
        origin = line_of(step) * columns + lax.rem(shot_here + devices - step, columns)
        return pltpu.make_async_remote_copy(
            src_ref=target.at[origin],
            dst_ref=target.at[origin],
            send_sem=send.at[which, step],
            recv_sem=recv.at[which, step],
            device_id={"xline": origin // columns, "shot": lax.rem(origin, columns)},
            device_id_type=mesh_id,
        )

    def along_line(which, source, target, step):
        peer = lax.rem(line + step, lines)
        return pltpu.make_async_remote_copy(
            src_ref=source.at[peer] if which else source,
            dst_ref=target.at[line],
            send_sem=line_send.at[which, step],
            recv_sem=line_recv.at[which, step],
            device_id={"xline": peer},
            device_id_type=mesh_id,
        )

    def from_line(which, target, step):
        origin = lax.rem(line + lines - step, lines)
        return pltpu.make_async_remote_copy(
            src_ref=target.at[origin],
            dst_ref=target.at[origin],
            send_sem=line_send.at[which, step],
            recv_sem=line_recv.at[which, step],
            device_id={"xline": origin},
            device_id_type=mesh_id,
        )

    def begin(step, _):
        copy_of(0, spectra_ref, spectra_out, step).start()
        return 0

    for step in range(1, lines):
        along_line(0, aperture_ref, apertures, step).start()
    lax.fori_loop(1, 2 * columns, begin, 0)
    mine = [
        pltpu.make_async_copy(aperture_ref, apertures.at[line], own.at[0]),
        pltpu.make_async_copy(spectra_ref.at[me], spectra_out.at[me], own.at[1]),
    ]
    for copy in mine:
        copy.start()
    for copy in mine:
        copy.wait()
    for step in range(1, lines):
        from_line(0, apertures, step).wait_recv()

    wanted = []
    for l in range(lines):
        wanted += [apertures[l, s : s + 1, :] for s in range(shots)]
        if width > shots * gathers:
            wanted.append(jnp.zeros((1, width - shots * gathers), jnp.int32))
    wanted = jnp.concatenate(wanted, axis=1)
    lane = lax.broadcasted_iota(jnp.int32, (receivers, lines * width), 1)
    receiver = lax.broadcasted_iota(jnp.int32, (receivers, lines * width), 0)
    total = jnp.zeros((time_rows, lines * width), jnp.float32)
    for shot in range(shots):
        hit = (lane % width // gathers == shot) & (receiver == wanted)
        onehot = jnp.where(hit, 1.0, 0.0).astype(jnp.bfloat16)
        total += jnp.dot(targets_ref[shot], onehot, preferred_element_type=jnp.float32)
    total = total.astype(jnp.bfloat16)
    for l in range(lines):
        traces_here[l] = total[:, l * width : (l + 1) * width]

    arrival_of(0, spectra_out, 1).wait_recv()
    for step in range(1, lines):
        along_line(1, traces_here, traces, step).start()
    lax.fori_loop(2 * columns, devices, begin, 0)
    keep = pltpu.make_async_copy(traces_here.at[line], traces.at[line], own.at[2])
    keep.start()
    keep.wait()
    for step in range(1, lines):
        from_line(1, traces, step).wait_recv()

    value = jnp.zeros((table_ref.shape[1], width), jnp.float32)
    for l in range(lines):
        value += lax.dot_general(
            table_ref[l * time_rows : (l + 1) * time_rows, :], traces[l],
            (((0,), (0,)), ((), ())),
            preferred_element_type=jnp.float32,
        )
    picked[...] = value.astype(jnp.bfloat16).reshape(picked.shape)
    arrival_of(0, spectra_out, 2).wait_recv()

    def begin_picked(step, _):
        copy_of(1, picked, picked_out, step).start()
        return 0

    lax.fori_loop(1, devices, begin_picked, 0)
    keep = pltpu.make_async_copy(picked.at[me], picked_out.at[me], own.at[3])
    keep.start()
    keep.wait()
    for step in range(1, lines):
        along_line(0, aperture_ref, apertures, step).wait_send()
        along_line(1, traces_here, traces, step).wait_send()

    def finish(step, _):
        copy_of(0, spectra_ref, spectra_out, step).wait_send()
        copy_of(1, picked, picked_out, step).wait_send()
        arrival_of(1, picked_out, step).wait_recv()
        return 0

    def arrived(step, _):
        arrival_of(0, spectra_out, step).wait_recv()
        return 0

    lax.fori_loop(3, devices, arrived, 0)
    lax.fori_loop(1, devices, finish, 0)


def collect_kernel(lines, columns, running_ref, out_ref, send, recv, own):
    line = lax.axis_index("xline")
    me = lax.axis_index("shot")
    core_line = line + 1 - 2 * lax.rem(line, 2)
    far_line = lax.rem(line + lines // 2, lines)
    diagonal_line = lax.rem(core_line + lines // 2, lines)
    mesh_id = pl.DeviceIdType.MESH
    barrier = pltpu.get_barrier_semaphore()

    def greet(step, _):
        pl.semaphore_signal(
            barrier, inc=1, device_id={"shot": lax.rem(me + step, columns)}, device_id_type=mesh_id
        )
        return 0

    lax.fori_loop(1, columns, greet, 0)
    for peer in (core_line, far_line):
        pl.semaphore_signal(barrier, inc=1, device_id={"xline": peer}, device_id_type=mesh_id)
    pl.semaphore_wait(barrier, columns + 1)

    def across(step):
        peer = lax.rem(me + step, columns)
        return pltpu.make_async_remote_copy(
            src_ref=running_ref.at[peer],
            dst_ref=out_ref.at[line * columns + me],
            send_sem=send.at[0, step],
            recv_sem=recv.at[0, step],
            device_id={"shot": peer},
            device_id_type=mesh_id,
        )

    def onward(stage, source_line, peer_line, step):
        slot = source_line * columns + lax.rem(me + columns - step, columns)
        return pltpu.make_async_remote_copy(
            src_ref=out_ref.at[slot],
            dst_ref=out_ref.at[slot],
            send_sem=send.at[stage, step],
            recv_sem=recv.at[stage, step],
            device_id={"xline": peer_line},
            device_id_type=mesh_id,
        )

    def begin(step, _):
        across(step).start()
        return 0

    lax.fori_loop(1, columns, begin, 0)
    mine = pltpu.make_async_copy(running_ref.at[me], out_ref.at[line * columns + me], own.at[0])
    mine.start()
    mine.wait()
    onward(2, line, far_line, 0).start()
    onward(1, line, core_line, 0).start()

    def relay(step, _):
        slot = line * columns + lax.rem(me + columns - step, columns)
        pltpu.make_async_remote_copy(
            src_ref=out_ref.at[slot],
            dst_ref=out_ref.at[slot],
            send_sem=send.at[0, step],
            recv_sem=recv.at[0, step],
            device_id={"shot": lax.rem(me + columns - step, columns)},
            device_id_type=mesh_id,
        ).wait_recv()
        onward(2, line, far_line, step).start()
        onward(1, line, core_line, step).start()
        return 0

    lax.fori_loop(1, columns, relay, 0)

    def turn(step, _):
        onward(2, far_line, far_line, step).wait_recv()
        onward(3, far_line, core_line, step).start()
        return 0

    lax.fori_loop(0, columns, turn, 0)

    def finish(step, _):
        onward(1, core_line, core_line, step).wait_recv()
        onward(3, diagonal_line, core_line, step).wait_recv()
        onward(1, line, core_line, step).wait_send()
        onward(2, line, far_line, step).wait_send()
        onward(3, far_line, core_line, step).wait_send()
        return 0

    lax.fori_loop(0, columns, finish, 0)

    def sent(step, _):
        across(step).wait_send()
        return 0

    lax.fori_loop(1, columns, sent, 0)


def xor_of(index, step):
    return lax.bitwise_xor(jnp.int32(index), jnp.int32(step))


def fused_kernel(
    lines, columns, bins,
    records_ref, targets_ref, aperture_ref, out_ref,
    records, table, inverse, expand, mixing, apertures, traces_here, traces,
    sent, spectra, picked_here, picked, running, gathered, raw, stage, unpacked,
    load, own, near_send, near_recv, wide_send, wide_recv, run_send, across_recv, far_recv, core_recv,
):
    f32, bf16 = jnp.float32, jnp.bfloat16
    devices = lines * columns
    halves = records.shape[0]
    time_rows, shots, receivers = targets_ref.shape
    held = records_ref.shape[0] // receivers
    part = receivers // halves
    gathers = aperture_ref.shape[1]
    chosen = shots * gathers
    width = 2 * chosen
    rows = columns * bins
    depth = 2 * bins
    line = lax.axis_index("xline")
    shot_here = lax.axis_index("shot")
    me = line * columns + shot_here
    mesh_id = pl.DeviceIdType.MESH
    barrier = pltpu.get_barrier_semaphore()

    def peer_at(step):
        near = lax.rem(step, 8)
        line_step = near // 4 * 2 + lax.rem(near, 2)
        shot_step = step // 8 * 2 + lax.rem(near // 2, 2)
        return xor_of(line, line_step), xor_of(shot_here, shot_step)

    def greet(j, _):
        peer_line, peer_shot = peer_at(devices - 1 - j)
        pl.semaphore_signal(
            barrier, inc=1,
            device_id={"xline": peer_line, "shot": peer_shot},
            device_id_type=mesh_id,
        )
        return 0

    lax.fori_loop(0, devices - 1, greet, 0)

    loads = []
    for h in range(halves):
        for g in range(held):
            loads.append(
                pltpu.make_async_copy(
                    records_ref.at[pl.ds(g * receivers + h * part, part), :],
                    records.at[h, pl.ds(g * part, part), :],
                    load.at[h, g],
                )
            )
    for copy in loads:
        copy.start()
    raw_load = pltpu.make_async_copy(targets_ref, raw, own.at[7])
    raw_load.start()
    aperture_load = pltpu.make_async_copy(aperture_ref, apertures.at[line], own.at[0])
    aperture_load.start()

    group = 4 * depth // 2
    scale = 1.0 / math.sqrt(NT)
    step_angle = 2.0 * math.pi / NT
    row = lax.broadcasted_iota(jnp.int32, (group, 128), 0)
    lane = lax.broadcasted_iota(jnp.int32, (group, 128), 1)
    freq = row // depth * bins + row % bins + 1
    turn = (row // bins % 2) * (NT // 4)
    group_bins = group // depth * bins

    def wave(first_freq, first_time):
        angle = ((freq + first_freq) * (lane + first_time) + turn) % NT
        return jnp.cos(angle.astype(f32) * step_angle) * scale

    across_time = 2.0 * jnp.cos((freq * 128 % NT).astype(f32) * step_angle)
    across_rows = 2.0 * jnp.cos((lane * group_bins % NT).astype(f32) * step_angle)
    flip = (1 - 2 * (freq % 2)).astype(f32)

    def fill(block, carry):
        at0, next0, at1, next1 = carry
        here = pl.ds(pl.multiple_of(block * group, group), group)
        now, later = at0, at1
        for k in range(NT // 256):
            table[here, k * 128 : (k + 1) * 128] = now.astype(bf16)
            table[here, NT // 2 + k * 128 : NT // 2 + (k + 1) * 128] = (now * flip).astype(bf16)
            now, later = later, across_time * later - now
        return next0, across_rows * next0 - at0, next1, across_rows * next1 - at1

    lax.fori_loop(
        0, 2 * NF // group, fill,
        (wave(0, 0), wave(group_bins, 0), wave(0, 128), wave(group_bins, 128)),
    )

    def transform(h):
        for g in range(held):
            loads[h * held + g].wait()
        value = lax.dot_general(
            table[...], records[h], (((1,), (1,)), ((), ())), preferred_element_type=f32
        )
        sent[h] = value.astype(bf16).reshape(sent.shape[1:])

    def await_all(source, target, count, send_sem, recv_sem):
        copy = pltpu.make_async_remote_copy(
            src_ref=source.at[pl.ds(0, count)],
            dst_ref=target.at[pl.ds(0, count)],
            send_sem=send_sem,
            recv_sem=recv_sem,
            device_id={"xline": xor_of(line, 1)},
            device_id_type=mesh_id,
        )
        copy.wait()

    def wide(which, source, target, step):
        peer_line, peer_shot = peer_at(step)
        return pltpu.make_async_remote_copy(
            src_ref=source.at[peer_line * columns + peer_shot],
            dst_ref=target.at[me],
            send_sem=wide_send.at[which],
            recv_sem=wide_recv.at[which],
            device_id={"xline": peer_line, "shot": peer_shot},
            device_id_type=mesh_id,
        )

    def wide_copy(which, step):
        if which < halves:
            return wide(which, sent.at[which], spectra.at[which], step)
        return wide(which, picked_here, picked, step)

    def start_wide(which, cross):
        def begin(j, _):
            wide_copy(which, (3 - j // 4) * 8 + cross * 4 + 3 - lax.rem(j, 4)).start()
            return 0

        lax.fori_loop(0, devices // 2 - 1 + cross, begin, 0)

    def wait_wide(which):
        if which < halves:
            source, target = sent.at[which], spectra.at[which]
        else:
            source, target = picked_here, picked
        await_all(source, target, devices - 1, wide_send.at[which], wide_recv.at[which])

    def along_line(which, step):
        peer = xor_of(line, step)
        source = traces_here.at[peer] if which else apertures.at[line]
        target = traces if which else apertures
        return pltpu.make_async_remote_copy(
            src_ref=source,
            dst_ref=target.at[line],
            send_sem=near_send.at[which * step],
            recv_sem=near_recv.at[which * step],
            device_id={"xline": peer},
            device_id_type=mesh_id,
        )

    def unpack_targets():
        raw_load.wait()
        rows = time_rows // 4
        for c in range(4):
            value = raw[c * rows : (c + 1) * rows].astype(f32)
            value = value.reshape(rows * shots, receivers)
            for h in range(halves):
                stage[h, c * rows * shots : (c + 1) * rows * shots, :] = value[:, h * part : (h + 1) * part]
        for shot in range(shots):
            for h in range(halves):
                unpacked[shot, :, h * part : (h + 1) * part] = (
                    stage[h, pl.ds(shot, time_rows, stride=shots), :].astype(bf16)
                )

    transform(0)
    unpack_targets()
    aperture_load.wait()
    pl.semaphore_wait(barrier, devices - 1)
    for step in range(1, lines):
        along_line(0, step).start()
    start_wide(0, 0)
    transform(1)
    start_wide(1, 0)
    mine = [
        pltpu.make_async_copy(sent.at[0, me], spectra.at[0, me], own.at[1]),
    ]
    for copy in mine:
        copy.start()
    keep_one = pltpu.make_async_copy(sent.at[1, me], spectra.at[1, me], own.at[2])
    keep_one.start()
    for copy in mine:
        copy.wait()
    await_all(apertures, apertures, lines - 1, near_send.at[0], near_recv.at[0])

    fold = time_rows // 2
    lane = lax.broadcasted_iota(jnp.int32, (fold, width), 1)
    receiver = lax.broadcasted_iota(jnp.int32, (receivers, width), 0)
    chosen_by = []
    for shot in range(shots):
        wanted = jnp.concatenate([apertures[l, shot : shot + 1, :] for l in range(lines)] * 2, axis=1)
        onehot = jnp.where(receiver == wanted, 1.0, 0.0).astype(bf16)
        value = jnp.dot(unpacked[shot], onehot, preferred_element_type=f32)
        chosen_by.append(jnp.where(lane < chosen, value[:fold], value[fold:]))
    for l in range(lines):
        value = chosen_by[l]
        for shot in range(shots):
            if shot != l:
                moved = pltpu.roll(chosen_by[shot], (shot - l) * gathers % width, 1)
                value = jnp.where(lane // gathers % shots == shot, moved, value)
        traces_here[l] = value.astype(bf16)
    for step in (2, 3, 1):
        along_line(1, step).start()
    keep = pltpu.make_async_copy(traces_here.at[line], traces.at[line], own.at[3])
    keep.start()
    start_wide(0, 1)
    taken = width
    across = held * columns * depth
    for shot in range(shots):
        for q in range(2):
            k = lax.broadcasted_iota(jnp.int32, (taken, held * columns * depth), 0)
            j = lax.broadcasted_iota(jnp.int32, (taken, held * columns * depth), 1)
            k_imag, k_shot, k_gather = k // chosen, k // gathers % shots, k % gathers
            j_held, j_column, j_imag = j // (columns * depth), j // depth % columns, j // bins % 2
            hit = (k_gather == j_column * held + j_held) & (k_shot == shot)
            hit = hit & ((k_imag != j_imag) if q else (k_imag == j_imag))
            value = jnp.where(hit, 1.0, 0.0)
            if q == 0:
                value = jnp.where(j_imag == 1, -value, value)
            expand[shot * 2 + q] = value.astype(bf16)
    slab = line * time_rows
    for c in range(time_rows // 128):
        block = table[:, pl.ds(pl.multiple_of(slab + c * 128, 128), 128)].astype(f32)
        inverse[c * 128 : (c + 1) * 128, :] = (block * 2.0).T.astype(bf16)


    keep.wait()
    ahead = jnp.zeros((2 * NF, width), f32)
    behind = jnp.zeros((2 * NF, width), f32)
    for step in range(lines):
        l = xor_of(line, step)
        if step:
            along_line(1, step).wait()
        base = pl.multiple_of(l * time_rows, time_rows)
        ahead += jnp.dot(table[:, pl.ds(base, fold)], traces[l], preferred_element_type=f32)
        behind += jnp.dot(table[:, pl.ds(base + fold, fold)], traces[l], preferred_element_type=f32)
    real = (ahead + pltpu.roll(behind, chosen, 1)).reshape(devices, depth, width)[:, :bins]
    imag = (pltpu.roll(ahead, chosen, 1) + behind).reshape(devices, depth, width)[:, bins:]
    lane = lax.broadcasted_iota(jnp.int32, (devices, bins, width), 2)
    picked_here[...] = jnp.where(lane < chosen, real, imag).astype(bf16)
    start_wide(2, 1)
    start_wide(2, 0)
    start_wide(1, 1)
    keep = pltpu.make_async_copy(picked_here.at[me], picked.at[me], own.at[4])
    keep.start()

    wait_wide(0)
    keep.wait()
    wait_wide(2)

    same_bin = (
        lax.broadcasted_iota(jnp.int32, (rows, across), 0) % bins
        == lax.broadcasted_iota(jnp.int32, (rows, across), 1) % bins
    )
    span = columns * depth
    for l in range(lines):
        block = picked[l * columns : (l + 1) * columns].astype(f32).reshape(rows, width).astype(bf16)
        for sq in range(2 * shots):
            value = jnp.dot(block, expand[sq], preferred_element_type=f32)
            value = jnp.where(same_bin, value, 0.0).astype(bf16)
            for g in range(held):
                first = (g * lines + l) * span
                mixing[sq * rows : (sq + 1) * rows, first : first + span] = (
                    value[:, g * span : (g + 1) * span]
                )

    def hop(h, stage, source_line, peer_line, step):
        slot = source_line * columns + xor_of(shot_here, step)
        return pltpu.make_async_remote_copy(
            src_ref=gathered.at[h, slot],
            dst_ref=gathered.at[h, slot],
            send_sem=run_send.at[h, stage],
            recv_sem=far_recv.at[h, step] if stage == 2 else core_recv.at[h, stage // 2],
            device_id={"xline": peer_line},
            device_id_type=mesh_id,
        )

    def spread(h, step):
        peer = xor_of(shot_here, step)
        return pltpu.make_async_remote_copy(
            src_ref=running.at[h, peer],
            dst_ref=gathered.at[h, me],
            send_sem=run_send.at[h, 0],
            recv_sem=across_recv.at[h, step],
            device_id={"shot": peer},
            device_id_type=mesh_id,
        )

    core_line = xor_of(line, 1)
    far_line = xor_of(line, 2)
    diagonal_line = xor_of(line, 3)

    def mix(h):
        total = jnp.zeros((2 * shots * rows, part), f32)
        for g in range(held):
            block = spectra[h, :, :, g * part : (g + 1) * part].reshape(2 * NF, part)
            total += jnp.dot(
                mixing[:, g * 2 * NF : (g + 1) * 2 * NF], block, preferred_element_type=f32
            )
        for column in range(columns):
            for shot in range(shots):
                pieces = [
                    total[(shot * 2 + q) * rows + column * bins :][:bins] for q in range(2)
                ]
                running[h, column, shot] = jnp.concatenate(pieces, axis=0).astype(bf16)

        def begin(j, _):
            spread(h, lax.select(j == 0, 1, columns - j)).start()
            return 0

        lax.fori_loop(0, columns - 1, begin, 0)
        keep = pltpu.make_async_copy(running.at[h, shot_here], gathered.at[h, me], own.at[5 + h])
        keep.start()
        keep.wait()
        hop(h, 2, line, far_line, 0).start()
        hop(h, 1, line, core_line, 0).start()

    def relay(h):
        def pass_on(j, _):
            step = lax.select(j == 0, 1, columns - j)
            spread(h, step).wait_recv()
            hop(h, 2, line, far_line, step).start()
            hop(h, 1, line, core_line, step).start()
            return 0

        lax.fori_loop(0, columns - 1, pass_on, 0)

    def turn_over(h):
        def pass_on(step, _):
            hop(h, 2, far_line, far_line, step).wait_recv()
            hop(h, 3, far_line, core_line, step).start()
            return 0

        lax.fori_loop(0, columns, pass_on, 0)

    def complete(h):
        def settled(stage, count):
            source = running.at[h, pl.ds(0, count)]
            return pltpu.make_async_remote_copy(
                src_ref=source,
                dst_ref=gathered.at[h, pl.ds(0, count)],
                send_sem=run_send.at[h, stage],
                recv_sem=core_recv.at[h, stage // 2],
                device_id={"xline": core_line},
                device_id_type=mesh_id,
            )

        settled(1, columns).wait()
        settled(3, columns).wait()
        settled(2, columns).wait_send()
        settled(0, columns - 1).wait_send()

    def invert(h):
        for shot in range(shots):
            block = gathered[h, :, shot].reshape(2 * NF, part)
            stage[h, pl.ds(shot, time_rows, stride=shots), :] = jnp.dot(
                inverse[...], block, preferred_element_type=f32
            )

    pieces = 4

    def emit(h):
        rows = time_rows // pieces
        lanes = slice(h * part, (h + 1) * part)
        for c in range(pieces):
            value = stage[h, c * rows * shots : (c + 1) * rows * shots, :]
            out_ref[c * rows : (c + 1) * rows, :, lanes] = value.reshape(rows, shots, part).astype(bf16)

    mix(0)
    keep_one.wait()
    wait_wide(1)
    mix(1)
    relay(0)
    relay(1)
    turn_over(0)
    turn_over(1)
    complete(0)
    invert(0)
    emit(0)
    complete(1)
    invert(1)
    emit(1)


def fused(records, targets, aperture):
    bf16 = jnp.bfloat16
    lines = lax.axis_size("xline")
    columns = lax.axis_size("shot")
    devices = lines * columns
    bins = NF // devices
    time_rows, shots, receivers = targets.shape
    held = records.shape[1]
    gathers = aperture.shape[2]
    halves, part = 2, receivers // 2
    width = 2 * shots * gathers
    wide = held * columns * 2 * bins
    stay = lambda array: pltpu.with_memory_space_constraint(array, pltpu.HBM)
    in_vmem = pl.BlockSpec(memory_space=pltpu.VMEM)
    in_hbm = pl.BlockSpec(memory_space=pltpu.HBM)
    dma = pltpu.SemaphoreType.DMA
    vmem = lambda *shape: pltpu.VMEM(shape, bf16)
    out = pl.pallas_call(
        functools.partial(fused_kernel, lines, columns, bins),
        out_shape=jax.ShapeDtypeStruct((time_rows, shots, receivers), bf16),
        in_specs=[in_hbm, in_hbm, in_hbm],
        out_specs=in_vmem,
        scratch_shapes=[
            vmem(halves, held * part, NT),
            vmem(2 * NF, NT),
            vmem(time_rows, 2 * NF),
            vmem(2 * shots, width, wide),
            vmem(2 * shots * columns * bins, lines * wide),
            pltpu.VMEM((lines, shots, gathers), jnp.int32),
            vmem(lines, time_rows // 2, width),
            vmem(lines, time_rows // 2, width),
            vmem(halves, devices, 2 * bins, held * part),
            vmem(halves, devices, 2 * bins, held * part),
            vmem(devices, bins, width),
            vmem(devices, bins, width),
            vmem(halves, columns, shots, 2 * bins, part),
            vmem(halves, devices, shots, 2 * bins, part),
            vmem(time_rows, shots, receivers),
            pltpu.VMEM((halves, time_rows * shots, part), jnp.float32),
            vmem(shots, time_rows, receivers),
            dma((halves, held)), dma((8,)), dma((lines,)), dma((lines,)), dma((3,)), dma((3,)),
            dma((halves, 4)), dma((halves, columns)), dma((halves, columns)), dma((halves, 2)),
        ],
        compiler_params=pltpu.CompilerParams(collective_id=2, has_side_effects=True, vmem_limit_bytes=24 << 20),
    )(stay(records.reshape(held * receivers, NT)), stay(targets), stay(aperture.reshape(shots, gathers)))
    return out


def on_device(records, targets, aperture):
    f32, bf16 = jnp.float32, jnp.bfloat16
    lines = lax.axis_size("xline")
    columns = lax.axis_size("shot")
    devices = lines * columns
    bins = NF // devices
    time_rows, shots, receivers = targets.shape
    held = records.shape[1]
    gathers = aperture.shape[2]
    if (lines, columns, bins, 2 * shots * gathers, receivers) == (4, 8, 8, 128, 256):
        return fused(records, targets, aperture)
    table = fourier_table(bins, 0, NT)
    chosen = shots * gathers
    padded = -(-chosen // 128) * 128

    spectra = jnp.einsum(
        "tp,kt->pk", table, records.reshape(held * receivers, NT), preferred_element_type=f32
    ).astype(bf16)

    spectra = spectra.reshape(devices, 2 * bins, held * receivers)
    in_vmem = pl.BlockSpec(memory_space=pltpu.VMEM)
    dma = pltpu.SemaphoreType.DMA
    spectra, picked = pl.pallas_call(
        functools.partial(spread_kernel, lines, columns, gathers),
        out_shape=[
            jax.ShapeDtypeStruct(spectra.shape, bf16),
            jax.ShapeDtypeStruct((devices, 2 * bins, padded), bf16),
        ],
        in_specs=[in_vmem] * 4,
        out_specs=[in_vmem] * 2,
        scratch_shapes=[
            pltpu.VMEM((lines, shots, gathers), jnp.int32),
            pltpu.VMEM((lines, time_rows, padded), bf16),
            pltpu.VMEM((lines, time_rows, padded), bf16),
            pltpu.VMEM((devices, 2 * bins, padded), bf16),
            dma((2, devices)), dma((2, devices)), dma((4,)), dma((2, lines)), dma((2, lines)),
        ],
        compiler_params=pltpu.CompilerParams(collective_id=0, has_side_effects=True),
    )(spectra, targets.transpose(1, 0, 2), aperture.reshape(shots, gathers), table)
    picked = picked.reshape(devices, 2, bins, padded)[..., :chosen]
    picked = jnp.concatenate([picked[:, 0], picked[:, 1]], axis=-1)

    running = pl.pallas_call(
        functools.partial(mix_kernel, lines, columns, held, bins, shots),
        out_shape=jax.ShapeDtypeStruct((shots * 2 * columns * bins, receivers), bf16),
        in_specs=[pl.BlockSpec(memory_space=pltpu.VMEM)] * 2,
        out_specs=pl.BlockSpec(memory_space=pltpu.VMEM),
    )(spectra.reshape(2 * NF, held * receivers), picked.reshape(NF, -1))
    running = running.reshape(shots, 2, columns, bins, receivers).transpose(2, 0, 1, 3, 4)
    running = running.reshape(columns, shots, 2 * bins, receivers)
    running = pl.pallas_call(
        functools.partial(collect_kernel, lines, columns),
        out_shape=jax.ShapeDtypeStruct((devices, *running.shape[1:]), bf16),
        in_specs=[in_vmem],
        out_specs=in_vmem,
        scratch_shapes=[dma((4, columns)), dma((4, columns)), dma((1,))],
        compiler_params=pltpu.CompilerParams(collective_id=1, has_side_effects=True),
    )(running)
    running = running.transpose(0, 2, 1, 3).reshape(2 * NF, shots, receivers)

    rows = fourier_table(bins, lax.axis_index("xline") * time_rows, time_rows)
    out = jnp.einsum("tp,psr->tsr", rows * 2, running, preferred_element_type=f32)
    return out.astype(bf16)


def solution(mesh):
    in_specs = (P("xline", "shot", None, None), P("xline", "shot", None), P("shot", "xline", None))
    out_specs = P("xline", "shot", None)
    return jax.shard_map(
        on_device, mesh=mesh, in_specs=in_specs, out_specs=out_specs, check_vma=False
    )
```

```python
import functools
import math

import jax
import jax.numpy as jnp
from jax import lax
from jax.experimental import pallas as pl
from jax.experimental.pallas import tpu as pltpu
from jax.sharding import PartitionSpec as P

NT = 2048
NF = 256
LOW = 32


def fourier_table(bins, start, count):
    blocks = NF // bins
    freq = jnp.arange(1, NF + 1, dtype=jnp.int32).reshape(blocks, 1, bins)
    freq = jnp.broadcast_to(freq, (blocks, 2, bins)).reshape(1, 2 * NF)
    is_imag = jnp.arange(2, dtype=jnp.int32).reshape(1, 2, 1)
    is_imag = jnp.broadcast_to(is_imag, (blocks, 2, bins)).reshape(1, 2 * NF) == 1

    def trig(times):
        angles = (times[:, None] * freq % NT).astype(jnp.float32) * (2.0 * math.pi / NT)
        return jnp.cos(angles), jnp.sin(angles)

    cos_hi, sin_hi = trig(start + jnp.arange(count // LOW, dtype=jnp.int32) * LOW)
    cos_lo, sin_lo = trig(jnp.arange(LOW, dtype=jnp.int32))
    scale = 1.0 / math.sqrt(NT)
    first = jnp.where(is_imag, -sin_hi, cos_hi) * scale
    second = jnp.where(is_imag, -cos_hi, -sin_hi) * scale
    first, second, cos_lo, sin_lo = lax.optimization_barrier((first, second, cos_lo, sin_lo))
    table = first[:, None] * cos_lo[None] + second[:, None] * sin_lo[None]
    return table.reshape(count, 2 * NF).astype(jnp.bfloat16)


def mix_kernel(lines, columns, held, bins, shots, spectra_ref, picked_ref, out_ref):
    gathers = columns * held
    receivers = out_ref.shape[1]
    rows = columns * bins
    depth = columns * 2 * bins
    taken = 2 * shots * gathers
    wide = held * depth

    k = lax.broadcasted_iota(jnp.int32, (taken, wide), 0)
    j = lax.broadcasted_iota(jnp.int32, (taken, wide), 1)
    k_imag, k_shot, k_gather = k // (shots * gathers), k // gathers % shots, k % gathers
    j_held, j_column, j_imag = j // depth, j % depth // (2 * bins), j // bins % 2
    same = k_gather == j_column * held + j_held
    crossed = k_imag != j_imag
    expand = []
    for shot in range(shots):
        for part in range(2):
            hit = same & (k_shot == shot) & (crossed if part else ~crossed)
            value = jnp.where(hit, 1.0, 0.0)
            if part == 0:
                value = jnp.where(j_imag == 1, -value, value)
            expand.append(value.astype(jnp.bfloat16))
    bin_of_row = lax.broadcasted_iota(jnp.int32, (rows, wide), 0) % bins
    bin_of_column = lax.broadcasted_iota(jnp.int32, (rows, wide), 1) % bins
    same_bin = bin_of_row == bin_of_column

    total = jnp.zeros(out_ref.shape, jnp.float32)
    for line in range(lines):
        block = picked_ref[line * rows : (line + 1) * rows, :]
        mixing = [
            jnp.where(
                same_bin, jnp.dot(block, matrix, preferred_element_type=jnp.float32), 0.0
            ).astype(jnp.bfloat16)
            for matrix in expand
        ]
        held_rows = slice(line * depth, (line + 1) * depth)
        spectra = jnp.concatenate(
            [spectra_ref[held_rows, h * receivers : (h + 1) * receivers] for h in range(held)], axis=0
        )
        total += jnp.dot(
            jnp.concatenate(mixing, axis=0), spectra, preferred_element_type=jnp.float32
        )
    out_ref[...] = total.astype(out_ref.dtype)


def spread_kernel(
    lines, columns, gathers, spectra_ref, targets_ref, aperture_ref, table_ref,
    spectra_out, picked_out,
    apertures, traces_here, traces, picked, send, recv, own, line_send, line_recv,
):
    devices = lines * columns
    line = lax.axis_index("xline")
    shot_here = lax.axis_index("shot")
    shots, time_rows, receivers = targets_ref.shape
    width = traces.shape[2]
    me = lax.axis_index("xline") * columns + lax.axis_index("shot")
    mesh_id = pl.DeviceIdType.MESH
    barrier = pltpu.get_barrier_semaphore()

    def greet(step, _):
        peer = lax.rem(me + step, devices)
        pl.semaphore_signal(
            barrier, inc=1,
            device_id={"xline": peer // columns, "shot": lax.rem(peer, columns)},
            device_id_type=mesh_id,
        )
        return 0

    lax.fori_loop(1, devices, greet, 0)
    pl.semaphore_wait(barrier, devices - 1)

    def line_of(step):
        far, other = step // columns // 2, lax.rem(step // columns, 2)
        moved = lax.rem(line + far * (lines // 2), lines)
        return moved + other * (1 - 2 * lax.rem(moved, 2))

    def copy_of(which, source, target, step):
        peer = line_of(step) * columns + lax.rem(shot_here + step, columns)
        return pltpu.make_async_remote_copy(
            src_ref=source.at[peer],
            dst_ref=target.at[me],
            send_sem=send.at[which, step],
            recv_sem=recv.at[which, step],
            device_id={"xline": peer // columns, "shot": lax.rem(peer, columns)},
            device_id_type=mesh_id,
        )

    def arrival_of(which, target, step):
        origin = line_of(step) * columns + lax.rem(shot_here + devices - step, columns)
        return pltpu.make_async_remote_copy(
            src_ref=target.at[origin],
            dst_ref=target.at[origin],
            send_sem=send.at[which, step],
            recv_sem=recv.at[which, step],
            device_id={"xline": origin // columns, "shot": lax.rem(origin, columns)},
            device_id_type=mesh_id,
        )

    def along_line(which, source, target, step):
        peer = lax.rem(line + step, lines)
        return pltpu.make_async_remote_copy(
            src_ref=source.at[peer] if which else source,
            dst_ref=target.at[line],
            send_sem=line_send.at[which, step],
            recv_sem=line_recv.at[which, step],
            device_id={"xline": peer},
            device_id_type=mesh_id,
        )

    def from_line(which, target, step):
        origin = lax.rem(line + lines - step, lines)
        return pltpu.make_async_remote_copy(
            src_ref=target.at[origin],
            dst_ref=target.at[origin],
            send_sem=line_send.at[which, step],
            recv_sem=line_recv.at[which, step],
            device_id={"xline": origin},
            device_id_type=mesh_id,
        )

    def begin(step, _):
        copy_of(0, spectra_ref, spectra_out, step).start()
        return 0

    for step in range(1, lines):
        along_line(0, aperture_ref, apertures, step).start()
    lax.fori_loop(1, 2 * columns, begin, 0)
    mine = [
        pltpu.make_async_copy(aperture_ref, apertures.at[line], own.at[0]),
        pltpu.make_async_copy(spectra_ref.at[me], spectra_out.at[me], own.at[1]),
    ]
    for copy in mine:
        copy.start()
    for copy in mine:
        copy.wait()
    for step in range(1, lines):
        from_line(0, apertures, step).wait_recv()

    wanted = []
    for l in range(lines):
        wanted += [apertures[l, s : s + 1, :] for s in range(shots)]
        if width > shots * gathers:
            wanted.append(jnp.zeros((1, width - shots * gathers), jnp.int32))
    wanted = jnp.concatenate(wanted, axis=1)
    lane = lax.broadcasted_iota(jnp.int32, (receivers, lines * width), 1)
    receiver = lax.broadcasted_iota(jnp.int32, (receivers, lines * width), 0)
    total = jnp.zeros((time_rows, lines * width), jnp.float32)
    for shot in range(shots):
        hit = (lane % width // gathers == shot) & (receiver == wanted)
        onehot = jnp.where(hit, 1.0, 0.0).astype(jnp.bfloat16)
        total += jnp.dot(targets_ref[shot], onehot, preferred_element_type=jnp.float32)
    total = total.astype(jnp.bfloat16)
    for l in range(lines):
        traces_here[l] = total[:, l * width : (l + 1) * width]

    arrival_of(0, spectra_out, 1).wait_recv()
    for step in range(1, lines):
        along_line(1, traces_here, traces, step).start()
    lax.fori_loop(2 * columns, devices, begin, 0)
    keep = pltpu.make_async_copy(traces_here.at[line], traces.at[line], own.at[2])
    keep.start()
    keep.wait()
    for step in range(1, lines):
        from_line(1, traces, step).wait_recv()

    value = jnp.zeros((table_ref.shape[1], width), jnp.float32)
    for l in range(lines):
        value += lax.dot_general(
            table_ref[l * time_rows : (l + 1) * time_rows, :], traces[l],
            (((0,), (0,)), ((), ())),
            preferred_element_type=jnp.float32,
        )
    picked[...] = value.astype(jnp.bfloat16).reshape(picked.shape)
    arrival_of(0, spectra_out, 2).wait_recv()

    def begin_picked(step, _):
        copy_of(1, picked, picked_out, step).start()
        return 0

    lax.fori_loop(1, devices, begin_picked, 0)
    keep = pltpu.make_async_copy(picked.at[me], picked_out.at[me], own.at[3])
    keep.start()
    keep.wait()
    for step in range(1, lines):
        along_line(0, aperture_ref, apertures, step).wait_send()
        along_line(1, traces_here, traces, step).wait_send()

    def finish(step, _):
        copy_of(0, spectra_ref, spectra_out, step).wait_send()
        copy_of(1, picked, picked_out, step).wait_send()
        arrival_of(1, picked_out, step).wait_recv()
        return 0

    def arrived(step, _):
        arrival_of(0, spectra_out, step).wait_recv()
        return 0

    lax.fori_loop(3, devices, arrived, 0)
    lax.fori_loop(1, devices, finish, 0)


def collect_kernel(lines, columns, running_ref, out_ref, send, recv, own):
    line = lax.axis_index("xline")
    me = lax.axis_index("shot")
    core_line = line + 1 - 2 * lax.rem(line, 2)
    far_line = lax.rem(line + lines // 2, lines)
    diagonal_line = lax.rem(core_line + lines // 2, lines)
    mesh_id = pl.DeviceIdType.MESH
    barrier = pltpu.get_barrier_semaphore()

    def greet(step, _):
        pl.semaphore_signal(
            barrier, inc=1, device_id={"shot": lax.rem(me + step, columns)}, device_id_type=mesh_id
        )
        return 0

    lax.fori_loop(1, columns, greet, 0)
    for peer in (core_line, far_line):
        pl.semaphore_signal(barrier, inc=1, device_id={"xline": peer}, device_id_type=mesh_id)
    pl.semaphore_wait(barrier, columns + 1)

    def across(step):
        peer = lax.rem(me + step, columns)
        return pltpu.make_async_remote_copy(
            src_ref=running_ref.at[peer],
            dst_ref=out_ref.at[line * columns + me],
            send_sem=send.at[0, step],
            recv_sem=recv.at[0, step],
            device_id={"shot": peer},
            device_id_type=mesh_id,
        )

    def onward(stage, source_line, peer_line, step):
        slot = source_line * columns + lax.rem(me + columns - step, columns)
        return pltpu.make_async_remote_copy(
            src_ref=out_ref.at[slot],
            dst_ref=out_ref.at[slot],
            send_sem=send.at[stage, step],
            recv_sem=recv.at[stage, step],
            device_id={"xline": peer_line},
            device_id_type=mesh_id,
        )

    def begin(step, _):
        across(step).start()
        return 0

    lax.fori_loop(1, columns, begin, 0)
    mine = pltpu.make_async_copy(running_ref.at[me], out_ref.at[line * columns + me], own.at[0])
    mine.start()
    mine.wait()
    onward(2, line, far_line, 0).start()
    onward(1, line, core_line, 0).start()

    def relay(step, _):
        slot = line * columns + lax.rem(me + columns - step, columns)
        pltpu.make_async_remote_copy(
            src_ref=out_ref.at[slot],
            dst_ref=out_ref.at[slot],
            send_sem=send.at[0, step],
            recv_sem=recv.at[0, step],
            device_id={"shot": lax.rem(me + columns - step, columns)},
            device_id_type=mesh_id,
        ).wait_recv()
        onward(2, line, far_line, step).start()
        onward(1, line, core_line, step).start()
        return 0

    lax.fori_loop(1, columns, relay, 0)

    def turn(step, _):
        onward(2, far_line, far_line, step).wait_recv()
        onward(3, far_line, core_line, step).start()
        return 0

    lax.fori_loop(0, columns, turn, 0)

    def finish(step, _):
        onward(1, core_line, core_line, step).wait_recv()
        onward(3, diagonal_line, core_line, step).wait_recv()
        onward(1, line, core_line, step).wait_send()
        onward(2, line, far_line, step).wait_send()
        onward(3, far_line, core_line, step).wait_send()
        return 0

    lax.fori_loop(0, columns, finish, 0)

    def sent(step, _):
        across(step).wait_send()
        return 0

    lax.fori_loop(1, columns, sent, 0)


def xor_of(index, step):
    return lax.bitwise_xor(jnp.int32(index), jnp.int32(step))


def fused_kernel(
    lines, columns, bins,
    records_ref, targets_ref, aperture_ref, out_ref,
    records, table, inverse, expand, mixing, apertures, traces_here, traces,
    sent, spectra, picked_here, picked, running, gathered, raw, stage, unpacked,
    load, own, near_send, near_recv, wide_send, wide_recv, run_send, across_recv, far_recv, core_recv,
):
    f32, bf16 = jnp.float32, jnp.bfloat16
    devices = lines * columns
    halves = records.shape[0]
    time_rows, shots, receivers = targets_ref.shape
    held = records_ref.shape[0] // receivers
    part = receivers // halves
    gathers = aperture_ref.shape[1]
    chosen = shots * gathers
    width = 2 * chosen
    rows = columns * bins
    depth = 2 * bins
    line = lax.axis_index("xline")
    shot_here = lax.axis_index("shot")
    me = line * columns + shot_here
    mesh_id = pl.DeviceIdType.MESH
    barrier = pltpu.get_barrier_semaphore()

    def peer_at(step):
        near = lax.rem(step, 8)
        line_step = near // 4 * 2 + lax.rem(near, 2)
        shot_step = step // 8 * 2 + lax.rem(near // 2, 2)
        return xor_of(line, line_step), xor_of(shot_here, shot_step)

    def greet(j, _):
        peer_line, peer_shot = peer_at(devices - 1 - j)
        pl.semaphore_signal(
            barrier, inc=1,
            device_id={"xline": peer_line, "shot": peer_shot},
            device_id_type=mesh_id,
        )
        return 0

    lax.fori_loop(0, devices - 1, greet, 0)

    loads = []
    for h in range(halves):
        for g in range(held):
            loads.append(
                pltpu.make_async_copy(
                    records_ref.at[pl.ds(g * receivers + h * part, part), :],
                    records.at[h, pl.ds(g * part, part), :],
                    load.at[h, g],
                )
            )
    for copy in loads:
        copy.start()
    raw_load = pltpu.make_async_copy(targets_ref, raw, own.at[7])
    raw_load.start()
    aperture_load = pltpu.make_async_copy(aperture_ref, apertures.at[line], own.at[0])
    aperture_load.start()

    group = 4 * depth // 2
    scale = 1.0 / math.sqrt(NT)
    step_angle = 2.0 * math.pi / NT
    row = lax.broadcasted_iota(jnp.int32, (group, 128), 0)
    lane = lax.broadcasted_iota(jnp.int32, (group, 128), 1)
    freq = row // depth * bins + row % bins + 1
    turn = (row // bins % 2) * (NT // 4)
    group_bins = group // depth * bins

    def wave(first_freq, first_time):
        angle = ((freq + first_freq) * (lane + first_time) + turn) % NT
        return jnp.cos(angle.astype(f32) * step_angle) * scale

    across_time = 2.0 * jnp.cos((freq * 128 % NT).astype(f32) * step_angle)
    across_rows = 2.0 * jnp.cos((lane * group_bins % NT).astype(f32) * step_angle)
    flip = (1 - 2 * (freq % 2)).astype(f32)

    def fill(block, carry):
        at0, next0, at1, next1 = carry
        here = pl.ds(pl.multiple_of(block * group, group), group)
        now, later = at0, at1
        for k in range(NT // 256):
            table[here, k * 128 : (k + 1) * 128] = now.astype(bf16)
            table[here, NT // 2 + k * 128 : NT // 2 + (k + 1) * 128] = (now * flip).astype(bf16)
            now, later = later, across_time * later - now
        return next0, across_rows * next0 - at0, next1, across_rows * next1 - at1

    lax.fori_loop(
        0, 2 * NF // group, fill,
        (wave(0, 0), wave(group_bins, 0), wave(0, 128), wave(group_bins, 128)),
    )

    def transform(h):
        for g in range(held):
            loads[h * held + g].wait()
        value = lax.dot_general(
            table[...], records[h], (((1,), (1,)), ((), ())), preferred_element_type=f32
        )
        sent[h] = value.astype(bf16).reshape(sent.shape[1:])

    def await_all(source, target, count, send_sem, recv_sem):
        copy = pltpu.make_async_remote_copy(
            src_ref=source.at[pl.ds(0, count)],
            dst_ref=target.at[pl.ds(0, count)],
            send_sem=send_sem,
            recv_sem=recv_sem,
            device_id={"xline": xor_of(line, 1)},
            device_id_type=mesh_id,
        )
        copy.wait()

    def wide(which, source, target, step):
        peer_line, peer_shot = peer_at(step)
        return pltpu.make_async_remote_copy(
            src_ref=source.at[peer_line * columns + peer_shot],
            dst_ref=target.at[me],
            send_sem=wide_send.at[which],
            recv_sem=wide_recv.at[which],
            device_id={"xline": peer_line, "shot": peer_shot},
            device_id_type=mesh_id,
        )

    def wide_copy(which, step):
        if which < halves:
            return wide(which, sent.at[which], spectra.at[which], step)
        return wide(which, picked_here, picked, step)

    def start_wide(which, cross):
        def begin(j, _):
            wide_copy(which, (3 - j // 4) * 8 + cross * 4 + 3 - lax.rem(j, 4)).start()
            return 0

        lax.fori_loop(0, devices // 2 - 1 + cross, begin, 0)

    def wait_wide(which):
        if which < halves:
            source, target = sent.at[which], spectra.at[which]
        else:
            source, target = picked_here, picked
        await_all(source, target, devices - 1, wide_send.at[which], wide_recv.at[which])

    def along_line(which, step):
        peer = xor_of(line, step)
        source = traces_here.at[peer] if which else apertures.at[line]
        target = traces if which else apertures
        return pltpu.make_async_remote_copy(
            src_ref=source,
            dst_ref=target.at[line],
            send_sem=near_send.at[which * step],
            recv_sem=near_recv.at[which * step],
            device_id={"xline": peer},
            device_id_type=mesh_id,
        )

    def unpack_targets():
        raw_load.wait()
        rows = time_rows // 4
        for c in range(4):
            value = raw[c * rows : (c + 1) * rows].astype(f32)
            value = value.reshape(rows * shots, receivers)
            for h in range(halves):
                stage[h, c * rows * shots : (c + 1) * rows * shots, :] = value[:, h * part : (h + 1) * part]
        for shot in range(shots):
            for h in range(halves):
                unpacked[shot, :, h * part : (h + 1) * part] = (
                    stage[h, pl.ds(shot, time_rows, stride=shots), :].astype(bf16)
                )

    transform(0)
    unpack_targets()
    aperture_load.wait()
    pl.semaphore_wait(barrier, devices - 1)
    for step in range(1, lines):
        along_line(0, step).start()
    start_wide(0, 1)
    start_wide(0, 0)
    transform(1)
    mine = [
        pltpu.make_async_copy(sent.at[0, me], spectra.at[0, me], own.at[1]),
    ]
    for copy in mine:
        copy.start()
    keep_one = pltpu.make_async_copy(sent.at[1, me], spectra.at[1, me], own.at[2])
    keep_one.start()
    for copy in mine:
        copy.wait()
    await_all(apertures, apertures, lines - 1, near_send.at[0], near_recv.at[0])

    fold = time_rows // 2
    lane = lax.broadcasted_iota(jnp.int32, (fold, width), 1)
    receiver = lax.broadcasted_iota(jnp.int32, (receivers, width), 0)
    chosen_by = []
    for shot in range(shots):
        wanted = jnp.concatenate([apertures[l, shot : shot + 1, :] for l in range(lines)] * 2, axis=1)
        onehot = jnp.where(receiver == wanted, 1.0, 0.0).astype(bf16)
        value = jnp.dot(unpacked[shot], onehot, preferred_element_type=f32)
        chosen_by.append(jnp.where(lane < chosen, value[:fold], value[fold:]))
    for l in range(lines):
        value = chosen_by[l]
        for shot in range(shots):
            if shot != l:
                moved = pltpu.roll(chosen_by[shot], (shot - l) * gathers % width, 1)
                value = jnp.where(lane // gathers % shots == shot, moved, value)
        traces_here[l] = value.astype(bf16)
    for step in (2, 3, 1):
        along_line(1, step).start()
    keep = pltpu.make_async_copy(traces_here.at[line], traces.at[line], own.at[3])
    keep.start()
    start_wide(1, 0)
    taken = width
    across = held * columns * depth
    for shot in range(shots):
        for q in range(2):
            k = lax.broadcasted_iota(jnp.int32, (taken, held * columns * depth), 0)
            j = lax.broadcasted_iota(jnp.int32, (taken, held * columns * depth), 1)
            k_imag, k_shot, k_gather = k // chosen, k // gathers % shots, k % gathers
            j_held, j_column, j_imag = j // (columns * depth), j // depth % columns, j // bins % 2
            hit = (k_gather == j_column * held + j_held) & (k_shot == shot)
            hit = hit & ((k_imag != j_imag) if q else (k_imag == j_imag))
            value = jnp.where(hit, 1.0, 0.0)
            if q == 0:
                value = jnp.where(j_imag == 1, -value, value)
            expand[shot * 2 + q] = value.astype(bf16)
    slab = line * time_rows
    for c in range(time_rows // 128):
        block = table[:, pl.ds(pl.multiple_of(slab + c * 128, 128), 128)].astype(f32)
        inverse[c * 128 : (c + 1) * 128, :] = (block * 2.0).T.astype(bf16)


    keep.wait()
    ahead = jnp.zeros((2 * NF, width), f32)
    behind = jnp.zeros((2 * NF, width), f32)
    for step in range(lines):
        l = xor_of(line, step)
        if step:
            along_line(1, step).wait()
        base = pl.multiple_of(l * time_rows, time_rows)
        ahead += jnp.dot(table[:, pl.ds(base, fold)], traces[l], preferred_element_type=f32)
        behind += jnp.dot(table[:, pl.ds(base + fold, fold)], traces[l], preferred_element_type=f32)
    real = (ahead + pltpu.roll(behind, chosen, 1)).reshape(devices, depth, width)[:, :bins]
    imag = (pltpu.roll(ahead, chosen, 1) + behind).reshape(devices, depth, width)[:, bins:]
    lane = lax.broadcasted_iota(jnp.int32, (devices, bins, width), 2)
    picked_here[...] = jnp.where(lane < chosen, real, imag).astype(bf16)
    start_wide(2, 1)
    start_wide(2, 0)
    start_wide(1, 1)
    keep = pltpu.make_async_copy(picked_here.at[me], picked.at[me], own.at[4])
    keep.start()

    wait_wide(0)
    keep.wait()
    wait_wide(2)

    same_bin = (
        lax.broadcasted_iota(jnp.int32, (rows, across), 0) % bins
        == lax.broadcasted_iota(jnp.int32, (rows, across), 1) % bins
    )
    span = columns * depth
    for l in range(lines):
        block = picked[l * columns : (l + 1) * columns].astype(f32).reshape(rows, width).astype(bf16)
        for sq in range(2 * shots):
            value = jnp.dot(block, expand[sq], preferred_element_type=f32)
            value = jnp.where(same_bin, value, 0.0).astype(bf16)
            for g in range(held):
                first = (g * lines + l) * span
                mixing[sq * rows : (sq + 1) * rows, first : first + span] = (
                    value[:, g * span : (g + 1) * span]
                )

    def hop(h, stage, source_line, peer_line, step):
        slot = source_line * columns + xor_of(shot_here, step)
        return pltpu.make_async_remote_copy(
            src_ref=gathered.at[h, slot],
            dst_ref=gathered.at[h, slot],
            send_sem=run_send.at[h, stage],
            recv_sem=far_recv.at[h, step] if stage == 2 else core_recv.at[h, stage // 2],
            device_id={"xline": peer_line},
            device_id_type=mesh_id,
        )

    def spread(h, step):
        peer = xor_of(shot_here, step)
        return pltpu.make_async_remote_copy(
            src_ref=running.at[h, peer],
            dst_ref=gathered.at[h, me],
            send_sem=run_send.at[h, 0],
            recv_sem=across_recv.at[h, step],
            device_id={"shot": peer},
            device_id_type=mesh_id,
        )

    core_line = xor_of(line, 1)
    far_line = xor_of(line, 2)
    diagonal_line = xor_of(line, 3)

    def mix(h):
        total = jnp.zeros((2 * shots * rows, part), f32)
        for g in range(held):
            block = spectra[h, :, :, g * part : (g + 1) * part].reshape(2 * NF, part)
            total += jnp.dot(
                mixing[:, g * 2 * NF : (g + 1) * 2 * NF], block, preferred_element_type=f32
            )
        for column in range(columns):
            for shot in range(shots):
                pieces = [
                    total[(shot * 2 + q) * rows + column * bins :][:bins] for q in range(2)
                ]
                running[h, column, shot] = jnp.concatenate(pieces, axis=0).astype(bf16)

        def begin(j, _):
            spread(h, j + 1).start()
            return 0

        lax.fori_loop(0, columns - 1, begin, 0)
        keep = pltpu.make_async_copy(running.at[h, shot_here], gathered.at[h, me], own.at[5 + h])
        keep.start()
        keep.wait()
        hop(h, 2, line, far_line, 0).start()
        hop(h, 1, line, core_line, 0).start()

    def relay(h):
        def pass_on(j, _):
            step = j + 1
            spread(h, step).wait_recv()
            hop(h, 2, line, far_line, step).start()
            hop(h, 1, line, core_line, step).start()
            return 0

        lax.fori_loop(0, columns - 1, pass_on, 0)

    def turn_over(h):
        def pass_on(step, _):
            hop(h, 2, far_line, far_line, step).wait_recv()
            hop(h, 3, far_line, core_line, step).start()
            return 0

        lax.fori_loop(0, columns, pass_on, 0)

    def complete(h, far):
        def settled(stage, count):
            source = running.at[h, pl.ds(0, count)]
            return pltpu.make_async_remote_copy(
                src_ref=source,
                dst_ref=gathered.at[h, pl.ds(0, count)],
                send_sem=run_send.at[h, stage],
                recv_sem=core_recv.at[h, stage // 2],
                device_id={"xline": core_line},
                device_id_type=mesh_id,
            )

        if far:
            settled(3, columns).wait()
            settled(2, columns).wait_send()
            settled(0, columns - 1).wait_send()
        else:
            settled(1, columns).wait()

    def invert(h, far):
        side = line // 2 + far * (1 - line // 2 * 2)
        first = pl.multiple_of(side * NF, NF)
        origin = side * (devices // 2)
        for shot in range(shots):
            block = gathered[h, pl.ds(origin, devices // 2), shot].reshape(NF, part)
            value = jnp.dot(inverse[:, pl.ds(first, NF)], block, preferred_element_type=f32)
            here = pl.ds(shot, time_rows, stride=shots)
            if far:
                value += stage[h, here, :]
            stage[h, here, :] = value

    pieces = 4

    def emit(h):
        rows = time_rows // pieces
        lanes = slice(h * part, (h + 1) * part)
        for c in range(pieces):
            value = stage[h, c * rows * shots : (c + 1) * rows * shots, :]
            out_ref[c * rows : (c + 1) * rows, :, lanes] = value.reshape(rows, shots, part).astype(bf16)

    mix(0)
    keep_one.wait()
    wait_wide(1)
    mix(1)
    relay(0)
    relay(1)
    turn_over(0)
    complete(0, 0)
    invert(0, 0)
    turn_over(1)
    complete(1, 0)
    invert(1, 0)
    complete(0, 1)
    invert(0, 1)
    emit(0)
    complete(1, 1)
    invert(1, 1)
    emit(1)


def fused(records, targets, aperture):
    bf16 = jnp.bfloat16
    lines = lax.axis_size("xline")
    columns = lax.axis_size("shot")
    devices = lines * columns
    bins = NF // devices
    time_rows, shots, receivers = targets.shape
    held = records.shape[1]
    gathers = aperture.shape[2]
    halves, part = 2, receivers // 2
    width = 2 * shots * gathers
    wide = held * columns * 2 * bins
    stay = lambda array: pltpu.with_memory_space_constraint(array, pltpu.HBM)
    in_vmem = pl.BlockSpec(memory_space=pltpu.VMEM)
    in_hbm = pl.BlockSpec(memory_space=pltpu.HBM)
    dma = pltpu.SemaphoreType.DMA
    vmem = lambda *shape: pltpu.VMEM(shape, bf16)
    out = pl.pallas_call(
        functools.partial(fused_kernel, lines, columns, bins),
        out_shape=jax.ShapeDtypeStruct((time_rows, shots, receivers), bf16),
        in_specs=[in_hbm, in_hbm, in_hbm],
        out_specs=in_vmem,
        scratch_shapes=[
            vmem(halves, held * part, NT),
            vmem(2 * NF, NT),
            vmem(time_rows, 2 * NF),
            vmem(2 * shots, width, wide),
            vmem(2 * shots * columns * bins, lines * wide),
            pltpu.VMEM((lines, shots, gathers), jnp.int32),
            vmem(lines, time_rows // 2, width),
            vmem(lines, time_rows // 2, width),
            vmem(halves, devices, 2 * bins, held * part),
            vmem(halves, devices, 2 * bins, held * part),
            vmem(devices, bins, width),
            vmem(devices, bins, width),
            vmem(halves, columns, shots, 2 * bins, part),
            vmem(halves, devices, shots, 2 * bins, part),
            vmem(time_rows, shots, receivers),
            pltpu.VMEM((halves, time_rows * shots, part), jnp.float32),
            vmem(shots, time_rows, receivers),
            dma((halves, held)), dma((8,)), dma((lines,)), dma((lines,)), dma((3,)), dma((3,)),
            dma((halves, 4)), dma((halves, columns)), dma((halves, columns)), dma((halves, 2)),
        ],
        compiler_params=pltpu.CompilerParams(collective_id=2, has_side_effects=True, vmem_limit_bytes=24 << 20),
    )(stay(records.reshape(held * receivers, NT)), stay(targets), stay(aperture.reshape(shots, gathers)))
    return out


def on_device(records, targets, aperture):
    f32, bf16 = jnp.float32, jnp.bfloat16
    lines = lax.axis_size("xline")
    columns = lax.axis_size("shot")
    devices = lines * columns
    bins = NF // devices
    time_rows, shots, receivers = targets.shape
    held = records.shape[1]
    gathers = aperture.shape[2]
    if (lines, columns, bins, 2 * shots * gathers, receivers) == (4, 8, 8, 128, 256):
        return fused(records, targets, aperture)
    table = fourier_table(bins, 0, NT)
    chosen = shots * gathers
    padded = -(-chosen // 128) * 128

    spectra = jnp.einsum(
        "tp,kt->pk", table, records.reshape(held * receivers, NT), preferred_element_type=f32
    ).astype(bf16)

    spectra = spectra.reshape(devices, 2 * bins, held * receivers)
    in_vmem = pl.BlockSpec(memory_space=pltpu.VMEM)
    dma = pltpu.SemaphoreType.DMA
    spectra, picked = pl.pallas_call(
        functools.partial(spread_kernel, lines, columns, gathers),
        out_shape=[
            jax.ShapeDtypeStruct(spectra.shape, bf16),
            jax.ShapeDtypeStruct((devices, 2 * bins, padded), bf16),
        ],
        in_specs=[in_vmem] * 4,
        out_specs=[in_vmem] * 2,
        scratch_shapes=[
            pltpu.VMEM((lines, shots, gathers), jnp.int32),
            pltpu.VMEM((lines, time_rows, padded), bf16),
            pltpu.VMEM((lines, time_rows, padded), bf16),
            pltpu.VMEM((devices, 2 * bins, padded), bf16),
            dma((2, devices)), dma((2, devices)), dma((4,)), dma((2, lines)), dma((2, lines)),
        ],
        compiler_params=pltpu.CompilerParams(collective_id=0, has_side_effects=True),
    )(spectra, targets.transpose(1, 0, 2), aperture.reshape(shots, gathers), table)
    picked = picked.reshape(devices, 2, bins, padded)[..., :chosen]
    picked = jnp.concatenate([picked[:, 0], picked[:, 1]], axis=-1)

    running = pl.pallas_call(
        functools.partial(mix_kernel, lines, columns, held, bins, shots),
        out_shape=jax.ShapeDtypeStruct((shots * 2 * columns * bins, receivers), bf16),
        in_specs=[pl.BlockSpec(memory_space=pltpu.VMEM)] * 2,
        out_specs=pl.BlockSpec(memory_space=pltpu.VMEM),
    )(spectra.reshape(2 * NF, held * receivers), picked.reshape(NF, -1))
    running = running.reshape(shots, 2, columns, bins, receivers).transpose(2, 0, 1, 3, 4)
    running = running.reshape(columns, shots, 2 * bins, receivers)
    running = pl.pallas_call(
        functools.partial(collect_kernel, lines, columns),
        out_shape=jax.ShapeDtypeStruct((devices, *running.shape[1:]), bf16),
        in_specs=[in_vmem],
        out_specs=in_vmem,
        scratch_shapes=[dma((4, columns)), dma((4, columns)), dma((1,))],
        compiler_params=pltpu.CompilerParams(collective_id=1, has_side_effects=True),
    )(running)
    running = running.transpose(0, 2, 1, 3).reshape(2 * NF, shots, receivers)

    rows = fourier_table(bins, lax.axis_index("xline") * time_rows, time_rows)
    out = jnp.einsum("tp,psr->tsr", rows * 2, running, preferred_element_type=f32)
    return out.astype(bf16)


def solution(mesh):
    in_specs = (P("xline", "shot", None, None), P("xline", "shot", None), P("shot", "xline", None))
    out_specs = P("xline", "shot", None)
    return jax.shard_map(
        on_device, mesh=mesh, in_specs=in_specs, out_specs=out_specs, check_vma=False
    )
```
